768 devices in a mesh: seq: 96 (over x, z, core), batch: 8 (over y).
Axes of the slice: x: 4, y: 8, z: 12, core: 2. Of those that a mesh axis runs over, the one named last changes fastest.
Arguments:
- queries: bfloat16 [8, 12288, 1024], P('batch', 'seq'), may hold values from -6 to 6
- keys: bfloat16 [8, 12288, 1024], P('batch', 'seq'), may hold values from -6 to 6
- values: bfloat16 [8, 12288, 1024], P('batch', 'seq'), may hold values from -6 to 6
- gates: bfloat16 [8, 12288, 1024], P('batch', 'seq'), may hold values from -6 to 6
- out_grad: bfloat16 [8, 12288, 1024], P('batch', 'seq'), may hold values from -6 to 6
- w_out: bfloat16 [1024, 1024], replicated, may hold values from -0.1875 to 0.1875
- hist_lengths: int32 [8, 4], P('batch'), may hold values from 1 to 8192, 12288 in all within a row
Outputs:
- output: bfloat16 [8, 12288, 1024], P('batch', 'seq')
- grad_queries: bfloat16 [8, 12288, 1024], P('batch', 'seq')
- grad_keys: bfloat16 [8, 12288, 1024], P('batch', 'seq')
- grad_values: bfloat16 [8, 12288, 1024], P('batch', 'seq')
- grad_gates: bfloat16 [8, 12288, 1024], P('batch', 'seq')
- grad_weight: float32 [1024, 1024], P('batch')
The draws below stay inside these ranges and needn't reach their ends.
Inputs may be any that keep to these rules, and one draw needn't show every extreme that they name: `hist_lengths`: each group's 4 lengths sum to 12288, and the longest of each group is exactly 8192.
All inputs are finite; a program needn't handle non-finite values.
Results may differ from the reference program's by a relative error of at most 0.0058.
Values may be sent and summed in bfloat16 or wider, within the bound.
A program may use at most 64 MiB of HBM per device.

```python
import math
import jax
import jax.numpy as jnp
import numpy as np
from jax import lax

HEADS = 8
HEAD_DIM = 128
D = 1024
WINDOW = 256
TOK_DEV = 128
REACH = 2
SEQS = 4
TOKENS = 12288
HIST_MAX = 8192
GROUPS = 8


def steps_of(key, dims, split, smallest, largest):
    factor_of = 1.0
    for axis_at, blocks in split:
        draws = jax.random.uniform(jax.random.fold_in(jax.random.fold_in(key, 6), axis_at), (blocks,), jnp.float32, smallest / len(split), largest / len(split))
        factor_of = factor_of * jnp.repeat(jnp.exp(draws), dims[axis_at] // blocks).reshape((-1,) + (1,) * (len(dims) - 1 - axis_at))
    return factor_of


def length_profile(count, total, reach, lean):
    portions = [(1 << 20) // math.isqrt(standing ** lean) + 1 for standing in range(2, count + 1)]
    rest, counts = total - reach - (count - 1), [1] * (count - 1)
    while rest > 0:
        free = [i for i in range(count - 1) if counts[i] < reach]
        pool, left = sum([portions[i] for i in free]), rest
        for i in free:
            extra = min(reach - counts[i], max(1, left * portions[i] // pool), rest)
            counts[i] = counts[i] + extra
            rest = rest - extra
    return np.array([reach] + counts)


def uneven(stream_key, count, total, reach, skew):
    if count == 2:
        one = jax.random.randint(stream_key, (), max(1, total - reach), min(reach, total - 1) + 1)
        return jnp.stack([one, total - one])
    tallies = jnp.asarray(length_profile(count, total, reach, skew), jnp.int32)
    pairs = (count - 1) // 2
    donor, sink = tallies[1:1 + 2 * pairs:2], tallies[2:2 + 2 * pairs:2]
    slack = jnp.minimum(donor - 1, reach - sink)
    passed = jax.random.randint(jax.random.fold_in(stream_key, 1), (pairs,), 0, 1 << 20) % (slack + 1)
    tallies = tallies.at[1:1 + 2 * pairs:2].set(donor - passed).at[2:2 + 2 * pairs:2].set(sink + passed)
    return tallies[jax.random.permutation(jax.random.fold_in(stream_key, 2), count)]


def noise(stream_key, shape, deviation, reach, cuts=(), kind=jnp.bfloat16):
    factor_of = steps_of(stream_key, shape, cuts, -0.22, 0.18) if cuts else 1.0
    result = jax.random.normal(stream_key, shape, jnp.float32) * deviation * factor_of
    return jnp.minimum(jnp.maximum(result, -reach), reach).astype(kind)


def setup_inputs(seed: int = 0) -> dict:
    arg_keys = jax.random.split(jax.random.key(seed), 8)
    queries = noise(arg_keys[0], (GROUPS, TOKENS, D), 1.0, 6.0, ((0, 8), (1, 96)))
    keys = noise(arg_keys[1], (GROUPS, TOKENS, D), 1.0, 6.0, ((0, 8), (1, 96)))
    values = noise(arg_keys[2], (GROUPS, TOKENS, D), 1.0, 6.0, ((0, 8), (1, 96)))
    gates = noise(arg_keys[3], (GROUPS, TOKENS, D), 1.0, 6.0, ((0, 8), (1, 96)))
    out_grad = noise(arg_keys[4], (GROUPS, TOKENS, D), 1.0, 6.0, ((0, 8), (1, 96)))
    w_out = noise(arg_keys[5], (D, D), D ** -0.5, 0.1875)
    hist_lengths = jax.vmap(lambda own: uneven(own, SEQS, TOKENS, HIST_MAX, 2))(jax.random.split(arg_keys[6], GROUPS)).reshape((GROUPS, SEQS)).astype(jnp.int32)
    return dict(queries=queries, keys=keys, values=values, gates=gates, out_grad=out_grad, w_out=w_out, hist_lengths=hist_lengths)


def segment_start(positions, lengths):
    seg_ends = jnp.cumsum(lengths).astype(jnp.int32)
    seg_begins = (seg_ends - lengths).astype(jnp.int32)
    inside = (seg_begins[None, :] <= positions[:, None]) & (positions[:, None] < seg_ends[None, :])
    return lax.optimization_barrier(jnp.sum(jnp.where(inside, seg_begins[None, :], 0), axis=1)).astype(jnp.int32)

def silu_slope(scores):
    logistic = jax.nn.sigmoid(scores)
    return logistic * (1.0 + scores * (1.0 - logistic))

def causal_mask(query_pos, query_start, key_pos):
    inside = (key_pos[None, :] >= query_start[:, None]) & (key_pos[None, :] <= query_pos[:, None])
    return inside & (key_pos[None, :] > query_pos[:, None] - WINDOW)

def one_group(query_rows, key_rows, value_rows, gate_rows, grad_rows, w_out, lengths):
    block_rows = TOK_DEV
    span_rows = (REACH + 1) * TOK_DEV
    block_count = TOKENS // TOK_DEV
    score_scale = HEAD_DIM ** (-0.5)
    positions = jnp.arange(TOKENS + REACH * block_rows, dtype=jnp.int32)
    starts = segment_start(positions, lengths)
    zero_rows = jnp.zeros((REACH * block_rows, D), jnp.bfloat16)
    key_front = jnp.concatenate([zero_rows, key_rows], axis=0)
    value_front = jnp.concatenate([zero_rows, value_rows], axis=0)
    indices = jnp.arange(block_count, dtype=jnp.int32)

    def query_side(first):
        query_blk = lax.dynamic_slice_in_dim(query_rows, first, block_rows, 0).astype(jnp.float32).reshape(block_rows, HEADS, HEAD_DIM)
        key_win = lax.dynamic_slice_in_dim(key_front, first, span_rows, 0).astype(jnp.float32).reshape(span_rows, HEADS, HEAD_DIM)
        value_win = lax.dynamic_slice_in_dim(value_front, first, span_rows, 0).astype(jnp.float32).reshape(span_rows, HEADS, HEAD_DIM)
        query_pos = first + jnp.arange(block_rows, dtype=jnp.int32)
        key_pos = first - REACH * block_rows + jnp.arange(span_rows, dtype=jnp.int32)
        query_start = lax.dynamic_slice_in_dim(starts, first, block_rows, 0)
        scores = jnp.einsum('ihe,jhe->hij', query_blk, key_win) * score_scale
        allowed = causal_mask(query_pos, query_start, key_pos)[None]
        return (scores, allowed, key_win, value_win)

    def forward_block(index):
        first = index * block_rows
        scores, allowed, key_win, value_win = query_side(first)
        attention = jnp.where(allowed, jax.nn.silu(scores), 0.0).astype(jnp.bfloat16)
        return jnp.einsum('hij,jhe->ihe', attention.astype(jnp.float32), value_win).reshape(block_rows, D)
    mixed = lax.map(forward_block, indices).reshape(TOKENS, D)
    centered = mixed - lax.optimization_barrier(jnp.mean(mixed, axis=1, keepdims=True))
    inv_std = lax.rsqrt(lax.optimization_barrier(jnp.mean(centered * centered, axis=1, keepdims=True)) + 1e-05)
    normed = centered * inv_std
    hidden = (normed * gate_rows.astype(jnp.float32)).astype(jnp.bfloat16)
    output = jnp.dot(hidden, w_out, preferred_element_type=jnp.float32).astype(jnp.bfloat16)
    grad_hidden = jnp.dot(grad_rows, w_out.T, preferred_element_type=jnp.float32)
    grad_gates = (grad_hidden * normed).astype(jnp.bfloat16)
    grad_norm = grad_hidden * gate_rows.astype(jnp.float32)
    grad_mix = ((grad_norm - lax.optimization_barrier(jnp.mean(grad_norm, axis=1, keepdims=True)) - normed * lax.optimization_barrier(jnp.mean(grad_norm * normed, axis=1, keepdims=True))) * inv_std).astype(jnp.bfloat16)

    def query_grad_block(index):
        first = index * block_rows
        scores, allowed, key_win, value_win = query_side(first)
        mix_blk = lax.dynamic_slice_in_dim(grad_mix, first, block_rows, 0).astype(jnp.float32).reshape(block_rows, HEADS, HEAD_DIM)
        grad_attention = jnp.einsum('ihe,jhe->hij', mix_blk, value_win)
        grad_scores = jnp.where(allowed, grad_attention * silu_slope(scores) * score_scale, 0.0).astype(jnp.bfloat16)
        return jnp.einsum('hij,jhe->ihe', grad_scores.astype(jnp.float32), key_win).reshape(block_rows, D)
    grad_queries = lax.map(query_grad_block, indices).reshape(TOKENS, D).astype(jnp.bfloat16)
    query_back = jnp.concatenate([query_rows, zero_rows], axis=0)
    mix_back = jnp.concatenate([grad_mix, zero_rows], axis=0)

    def key_grad_block(index):
        first = index * block_rows
        key_blk = lax.dynamic_slice_in_dim(key_rows, first, block_rows, 0).astype(jnp.float32).reshape(block_rows, HEADS, HEAD_DIM)
        value_blk = lax.dynamic_slice_in_dim(value_rows, first, block_rows, 0).astype(jnp.float32).reshape(block_rows, HEADS, HEAD_DIM)
        query_win = lax.dynamic_slice_in_dim(query_back, first, span_rows, 0).astype(jnp.float32).reshape(span_rows, HEADS, HEAD_DIM)
        mix_win = lax.dynamic_slice_in_dim(mix_back, first, span_rows, 0).astype(jnp.float32).reshape(span_rows, HEADS, HEAD_DIM)
        query_pos = first + jnp.arange(span_rows, dtype=jnp.int32)
        query_start = lax.dynamic_slice_in_dim(starts, first, span_rows, 0)
        key_pos = first + jnp.arange(block_rows, dtype=jnp.int32)
        scores = jnp.einsum('ihe,jhe->hij', query_win, key_blk) * score_scale
        allowed = causal_mask(query_pos, query_start, key_pos)[None]
        attention = jnp.where(allowed, jax.nn.silu(scores), 0.0).astype(jnp.bfloat16)
        grad_attention = jnp.einsum('ihe,jhe->hij', mix_win, value_blk)
        grad_scores = jnp.where(allowed, grad_attention * silu_slope(scores) * score_scale, 0.0).astype(jnp.bfloat16)
        grad_key_blk = jnp.einsum('hij,ihe->jhe', grad_scores.astype(jnp.float32), query_win).reshape(block_rows, D)
        grad_value_blk = jnp.einsum('hij,ihe->jhe', attention.astype(jnp.float32), mix_win).reshape(block_rows, D)
        return (grad_key_blk, grad_value_blk)
    grad_key_all, grad_value_all = lax.map(key_grad_block, indices)
    grad_keys = grad_key_all.reshape(TOKENS, D).astype(jnp.bfloat16)
    grad_values = grad_value_all.reshape(TOKENS, D).astype(jnp.bfloat16)
    weight_term = lax.dot_general(hidden, grad_rows, (((0,), (0,)), ((), ())), preferred_element_type=jnp.float32)
    return (output, grad_queries, grad_keys, grad_values, grad_gates, weight_term)

def reference(queries, keys, values, gates, out_grad, w_out, hist_lengths):
    results = []
    weight_total = jnp.zeros((D, D), jnp.float32)
    for group in range(GROUPS):
        outcome = one_group(queries[group], keys[group], values[group], gates[group], out_grad[group], w_out, hist_lengths[group])
        results.append(outcome[:5])
        weight_total = weight_total + outcome[5]
    stacked = [jnp.stack([item[place] for item in results]) for place in range(5)]
    grad_weight = weight_total * (GROUPS * TOKENS) ** (-0.5)
    return (stacked[0], stacked[1], stacked[2], stacked[3], stacked[4], grad_weight)
```

```python
import functools

import jax
import jax.numpy as jnp
from jax import lax
from jax.experimental import pallas as pl
from jax.experimental.pallas import tpu as pltpu
from jax.sharding import PartitionSpec as P

HEADS = 8
WINDOW = 256
REACH = 2
NX, NY, NZ = 4, 8, 12
MESH = pl.DeviceIdType.MESH


def shifted(block, axis, distance):
    devices = range(lax.axis_size(axis))
    route = [(i - distance, i) for i in devices if i - distance in devices]
    return lax.ppermute(block, axis, route)


def segment_start(positions, lengths):
    seg_ends = jnp.cumsum(lengths)
    seg_begins = seg_ends - lengths
    inside = (seg_begins[None, :] <= positions[:, None]) & (positions[:, None] < seg_ends[None, :])
    return jnp.sum(jnp.where(inside, seg_begins[None, :], 0), axis=1)


def silu_slope(scores):
    logistic = jax.nn.sigmoid(scores)
    return logistic * (1.0 + scores * (1.0 - logistic))


def causal_mask(query_pos, query_start, key_pos):
    inside = (key_pos[None, :] >= query_start[:, None]) & (key_pos[None, :] <= query_pos[:, None])
    return inside & (key_pos[None, :] > query_pos[:, None] - WINDOW)


def reduce_kernel(scale, g_ref, out_ref, sc, rc, s0, rx, s1, ry, s2, rz, ag, fin, send_sem, rc_sem, rx_sem, ry_sem, rz_sem, ag_sem, fin_sem):
    f32, bf16 = jnp.float32, jnp.bfloat16
    seq = lax.axis_index("seq")
    y = lax.axis_index("batch")
    k = lax.rem(seq, 2)
    x = seq // (2 * NZ)
    z = lax.rem(seq // 2, NZ)

    def dev(px, py, pz, pk):
        return {"seq": (px * NZ + pz) * 2 + pk, "batch": py}

    partner = dev(x, y, z, 1 - k)
    xs = [dev(lax.rem(x + d, NX), y, z, k) for d in range(1, NX)]
    xo = [dev(lax.rem(x + d, NX), y, z, 1 - k) for d in range(1, NX)]
    ys = [dev(x, lax.rem(y + d, NY), z, k) for d in range(1, NY)]
    zs = [dev(x, y, lax.rem(z + d, NZ), k) for d in range(1, NZ)]
    barrier = pltpu.get_barrier_semaphore()
    everyone = [partner] + xs + xo + ys + zs
    for peer in everyone:
        pl.semaphore_signal(barrier, inc=1, device_id=peer, device_id_type=MESH)

    sends = []

    def send(src, dst, recv_sem, peer):
        copy = pltpu.make_async_remote_copy(
            src_ref=src, dst_ref=dst, send_sem=send_sem.at[len(sends)], recv_sem=recv_sem,
            device_id=peer, device_id_type=MESH)
        copy.start()
        sends.append(copy)
        return copy

    other = pl.multiple_of((1 - k) * 512, 512)
    own = pl.multiple_of(k * 512, 512)
    sc[...] = g_ref[:, pl.ds(other, 512)].astype(bf16)
    pl.semaphore_wait(barrier, len(everyone))

    c = send(sc, rc, rc_sem, partner)
    c.wait_recv()
    for j in range(NX):
        for i in range(NY):
            rows = pl.ds(i * 128 + j * 32, 32)
            s0[j, i] = (g_ref[rows, pl.ds(own, 512)] + rc[rows, :].astype(f32)).astype(bf16)

    cs = [send(s0.at[lax.rem(x + d, NX)], rx.at[d - 1], rx_sem.at[d - 1], xs[d - 1]) for d in range(1, NX)]
    for c in cs:
        c.wait_recv()
    for i in range(NY):
        t = s0[x, i].astype(f32)
        for d in range(NX - 1):
            t = t + rx[d, i].astype(f32)
        s1[i] = t.astype(bf16)

    cs = [send(s1.at[lax.rem(y + d, NY)], ry.at[d - 1], ry_sem.at[d - 1], ys[d - 1]) for d in range(1, NY)]
    for c in cs:
        c.wait_recv()
    t = s1[y].astype(f32)
    for d in range(NY - 1):
        t = t + ry[d].astype(f32)
    for r in range(2):
        for j in range(4):
            s2[r * 4 + j] = t[r * 16:r * 16 + 16, j * 128:j * 128 + 128].astype(bf16)
    s2[8:] = jnp.zeros((NZ - 8, 16, 128), bf16)

    cs = [send(s2.at[lax.rem(z + d, NZ)], rz.at[d - 1], rz_sem.at[d - 1], zs[d - 1]) for d in range(1, NZ)]
    for c in cs:
        c.wait_recv()
    t = s2[z].astype(f32)
    for d in range(NZ - 1):
        t = t + rz[d].astype(f32)
    ag[z] = t.astype(bf16)
    cs = [send(ag.at[z], ag.at[z], ag_sem.at[d - 1], zs[d - 1]) for d in range(1, NZ)]
    for c in cs:
        c.wait_recv()

    slot = x * 2 + k
    fin[slot] = ag[0:8]
    peers = [partner] + xs + xo
    cs = [send(ag.at[pl.ds(0, 8)], fin.at[slot], fin_sem.at[i], p) for i, p in enumerate(peers)]
    for c in cs:
        c.wait_recv()
    for px in range(NX):
        for pk in range(2):
            for r in range(2):
                for j in range(4):
                    out_ref[px * 32 + r * 16:px * 32 + r * 16 + 16, pk * 512 + j * 128:pk * 512 + j * 128 + 128] = (
                        fin[px * 2 + pk, r * 4 + j].astype(f32) * scale)
    for c in sends:
        c.wait_send()


def reduce_weight(g, scale):
    bf16 = jnp.bfloat16
    vm = pltpu.VMEM
    dma = pltpu.SemaphoreType.DMA
    n_sends = 1 + (NX - 1) + (NY - 1) + 2 * (NZ - 1) + 7
    return pl.pallas_call(
        functools.partial(reduce_kernel, scale),
        out_shape=jax.ShapeDtypeStruct((128, 1024), jnp.float32),
        in_specs=[pl.BlockSpec(memory_space=pltpu.VMEM)],
        out_specs=pl.BlockSpec(memory_space=pltpu.VMEM),
        scratch_shapes=[
            vm((1024, 512), bf16), vm((1024, 512), bf16),
            vm((NX, NY, 32, 512), bf16), vm((NX - 1, NY, 32, 512), bf16),
            vm((NY, 32, 512), bf16), vm((NY - 1, 32, 512), bf16),
            vm((NZ, 16, 128), bf16), vm((NZ - 1, 16, 128), bf16),
            vm((NZ, 16, 128), bf16), vm((8, 8, 16, 128), bf16),
            dma((n_sends,)), dma, dma((NX - 1,)), dma((NY - 1,)), dma((NZ - 1,)), dma((NZ - 1,)), dma((7,)),
        ],
        compiler_params=pltpu.CompilerParams(collective_id=0, has_side_effects=True, vmem_limit_bytes=40 << 20),
    )(g)


def on_device(queries, keys, values, gates, out_grad, w_out, hist_lengths):
    query_rows = queries[0]
    key_rows = keys[0]
    value_rows = values[0]
    gate_rows = gates[0]
    grad_rows = out_grad[0]
    lengths = hist_lengths[0]
    row_total, model_width = query_rows.shape
    head_dim = model_width // HEADS
    score_scale = head_dim ** (-0.5)
    device = lax.axis_index("seq")
    local_iota = jnp.arange(row_total, dtype=jnp.int32)
    local_pos = device * row_total + local_iota
    local_start = segment_start(local_pos, lengths)
    stacked = jnp.stack((key_rows, value_rows))
    panels = [stacked]
    current = stacked
    for distance in range(REACH):
        current = shifted(current, "seq", 1)
        panels.append(current)
    window = jnp.concatenate(panels, axis=1)
    key_pos = jnp.concatenate(
        [(device - distance) * row_total + local_iota for distance in range(REACH + 1)]
    )
    key_heads = window[0].reshape(-1, HEADS, head_dim)
    value_heads = window[1].reshape(-1, HEADS, head_dim)
    query_heads = query_rows.reshape(row_total, HEADS, head_dim)
    scores = (
        jnp.einsum("ihe,jhe->hij", query_heads, key_heads, preferred_element_type=jnp.float32)
        * score_scale
    )
    allowed = causal_mask(local_pos, local_start, key_pos)[None]
    attention = jnp.where(allowed, jax.nn.silu(scores), 0.0).astype(jnp.bfloat16)
    mixed = jnp.einsum(
        "hij,jhe->ihe", attention, value_heads, preferred_element_type=jnp.float32
    ).reshape(row_total, model_width)
    centered = mixed - jnp.mean(mixed, axis=1, keepdims=True)
    inv_std = lax.rsqrt(jnp.mean(centered * centered, axis=1, keepdims=True) + 1e-05)
    normed = centered * inv_std
    hidden = (normed * gate_rows.astype(jnp.float32)).astype(jnp.bfloat16)
    output = jnp.dot(hidden, w_out, preferred_element_type=jnp.float32).astype(jnp.bfloat16)
    grad_hidden = lax.dot_general(
        grad_rows, w_out, (((1,), (1,)), ((), ())), preferred_element_type=jnp.float32
    )
    grad_gates = (grad_hidden * normed).astype(jnp.bfloat16)
    grad_norm = grad_hidden * gate_rows.astype(jnp.float32)
    grad_mix = (
        (
            grad_norm
            - jnp.mean(grad_norm, axis=1, keepdims=True)
            - normed * jnp.mean(grad_norm * normed, axis=1, keepdims=True)
        )
        * inv_std
    ).astype(jnp.bfloat16)
    mix_heads = grad_mix.reshape(row_total, HEADS, head_dim)
    grad_attention = jnp.einsum(
        "ihe,jhe->hij", mix_heads, value_heads, preferred_element_type=jnp.float32
    )
    grad_scores = jnp.where(allowed, grad_attention * silu_slope(scores) * score_scale, 0.0).astype(
        jnp.bfloat16
    )
    grad_queries = (
        jnp.einsum("hij,jhe->ihe", grad_scores, key_heads, preferred_element_type=jnp.float32)
        .reshape(row_total, model_width)
        .astype(jnp.bfloat16)
    )
    grad_key_all = jnp.einsum(
        "hij,ihe->jhe", grad_scores, query_heads, preferred_element_type=jnp.float32
    ).reshape(-1, model_width)
    grad_value_all = jnp.einsum(
        "hij,ihe->jhe", attention, mix_heads, preferred_element_type=jnp.float32
    ).reshape(-1, model_width)
    totals = jnp.stack((grad_key_all[:row_total], grad_value_all[:row_total]))
    for distance in range(1, REACH + 1):
        partial_grads = jnp.stack(
            (
                grad_key_all[distance * row_total : (distance + 1) * row_total],
                grad_value_all[distance * row_total : (distance + 1) * row_total],
            )
        )
        totals = totals + shifted(partial_grads, "seq", -distance)
    grad_keys = totals[0].astype(jnp.bfloat16)
    grad_values = totals[1].astype(jnp.bfloat16)
    token_total = row_total * lax.axis_size("seq") * lax.axis_size("batch")
    grad_weight = reduce_weight(
        lax.dot_general(
            hidden, grad_rows, (((0,), (0,)), ((), ())), preferred_element_type=jnp.float32
        ),
        token_total ** (-0.5),
    )
    return (
        output[None],
        grad_queries[None],
        grad_keys[None],
        grad_values[None],
        grad_gates[None],
        grad_weight,
    )


def solution(mesh):
    placed = (
        P("batch", "seq", None),
        P("batch", "seq", None),
        P("batch", "seq", None),
        P("batch", "seq", None),
        P("batch", "seq", None),
        P(),
        P("batch", None),
    )
    return jax.shard_map(
        on_device,
        mesh=mesh,
        in_specs=placed,
        out_specs=(
            P("batch", "seq", None),
            P("batch", "seq", None),
            P("batch", "seq", None),
            P("batch", "seq", None),
            P("batch", "seq", None),
            P("batch", None),
        ),
        check_vma=False,
    )
```

```python
import functools

import jax
import jax.numpy as jnp
from jax import lax
from jax.experimental import pallas as pl
from jax.experimental.pallas import tpu as pltpu
from jax.sharding import PartitionSpec as P

HEADS = 8
WINDOW = 256
NX, NY, NZ = 4, 8, 12
OWNERS = 8
NSEQ = NX * NZ * 2
MESH = pl.DeviceIdType.MESH
f32, bf16 = jnp.float32, jnp.bfloat16
LAST = (((1,), (1,)), ((), ()))
FIRST = (((0,), (0,)), ((), ()))


def dot(a, b, dims=(((1,), (0,)), ((), ()))):
    return lax.dot_general(a, b, dims, preferred_element_type=f32)


def layer_kernel(
    token_total, len_ref, q_hbm, k_hbm, v_hbm, u_hbm, og_hbm, w_hbm,
    out_ref, gq_ref, gk_ref, gv_ref, gg_ref, gw_ref,
    q, u, w, og8, kwin, vwin, maskf, slope, att, mixed, gh, gmix, inv, hid, ht, htr, gs, ry, s2, rz, ag, finr, go, pg, rg,
    ld_sem, ss_kv, rs_kv, ss_og, rs_og, ss_h, rs_h, ss_y, rs_y, ss_z, rs_z, ss_a, rs_a, ss_f, rs_f, ss_g, rs_g,
):
    seq = lax.axis_index("seq")
    y = lax.axis_index("batch")
    k = lax.rem(seq, 2)
    x = seq // (2 * NZ)
    z = lax.rem(seq // 2, NZ)
    me = x * 2 + k

    def dev(px, py, pz, pk):
        return {"seq": (px * NZ + pz) * 2 + pk, "batch": py}

    def ring(d):
        return {"seq": lax.rem(seq + d + NSEQ, NSEQ), "batch": y}

    partner = dev(x, y, z, 1 - k)
    xs = [dev(lax.rem(x + d, NX), y, z, k) for d in range(1, NX)]
    xo = [dev(lax.rem(x + d, NX), y, z, 1 - k) for d in range(1, NX)]
    ys = [dev(x, lax.rem(y + d, NY), z, k) for d in range(1, NY)]
    zs = [dev(x, y, lax.rem(z + d, NZ), k) for d in range(1, NZ)]
    xk = [partner] + xs + xo
    to_slab = [x * 2 + 1 - k] + [lax.rem(x + d, NX) * 2 + k for d in range(1, NX)] + [lax.rem(x + d, NX) * 2 + 1 - k for d in range(1, NX)]
    hops = [ring(-1), ring(1), ring(-2), ring(2)]

    barrier = pltpu.get_barrier_semaphore()
    greeted = xk + ys + zs + hops
    for peer in greeted:
        pl.semaphore_signal(barrier, inc=1, device_id=peer, device_id_type=MESH)

    def remote(src, dst, ss, rs, peer):
        return pltpu.make_async_remote_copy(src_ref=src, dst_ref=dst, send_sem=ss, recv_sem=rs, device_id=peer, device_id_type=MESH)

    def lanes(h):
        return pl.ds(pl.multiple_of(h * 128, 128), 128)

    loads = [
        pltpu.make_async_copy(q_hbm.at[0], q, ld_sem.at[0]),
        pltpu.make_async_copy(og_hbm.at[0], og8.at[me], ld_sem.at[1]),
        pltpu.make_async_copy(w_hbm, w, ld_sem.at[2]),
        pltpu.make_async_copy(u_hbm.at[0], u, ld_sem.at[3]),
    ]
    for h in range(HEADS):
        loads.append(pltpu.make_async_copy(k_hbm.at[0, :, pl.ds(h * 128, 128)], kwin.at[h, pl.ds(256, 128)], ld_sem.at[4 + 2 * h]))
        loads.append(pltpu.make_async_copy(v_hbm.at[0, :, pl.ds(h * 128, 128)], vwin.at[h, pl.ds(256, 128)], ld_sem.at[5 + 2 * h]))
    for c in loads:
        c.start()
    pl.semaphore_wait(barrier, len(greeted))

    def kv_far(h, which):
        src, dst = ((k_hbm, kwin), (v_hbm, vwin))[which]
        return remote(src.at[0, :, lanes(h)], dst.at[h, pl.ds(0, 128)], ss_kv.at[0, h, which], rs_kv.at[0, h, which], ring(2))

    def kv_near(h, which):
        src, dst = ((k_hbm, kwin), (v_hbm, vwin))[which]
        return remote(src.at[0, :, lanes(h)], dst.at[h, pl.ds(128, 128)], ss_kv.at[1, h, which], rs_kv.at[1, h, which], partner)

    def kv_relay(h, which):
        dst = (kwin, vwin)[which]
        return remote(dst.at[h, pl.ds(0, 128)], dst.at[h, pl.ds(128, 128)], ss_kv.at[1, h, which], rs_kv.at[1, h, which], partner)

    for h in range(HEADS):
        for which in range(2):
            kv_far(h, which).start()

    @pl.when(k == 0)
    def _():
        for h in range(HEADS):
            for which in range(2):
                kv_near(h, which).start()

    og_sends = [remote(og_hbm.at[0], og8.at[me], ss_og.at[d - 1], rs_og.at[d - 1], xs[d - 1]) for d in range(1, NX)]
    og_sends.append(remote(og_hbm.at[0], og8.at[me], ss_og.at[3], rs_og.at[3], partner))
    for c in og_sends:
        c.start()

    loads[1].wait()
    loads[2].wait()
    gh[...] = dot(og8[me], w[...], LAST)
    b1 = len_ref[0, 0]
    b2 = b1 + len_ref[0, 1]
    b3 = b2 + len_ref[0, 2]
    base = seq * 128
    pos = base + lax.broadcasted_iota(jnp.int32, (128, 384), 0)
    key_pos = base - 256 + lax.broadcasted_iota(jnp.int32, (128, 384), 1)
    start = jnp.where(pos >= b3, b3, jnp.where(pos >= b2, b2, jnp.where(pos >= b1, b1, 0)))
    allowed = (key_pos >= start) & (key_pos <= pos) & (key_pos > pos - WINDOW)
    maskf[...] = jnp.where(allowed, 1.0, 0.0)
    loads[0].wait()
    for c in loads[3:]:
        c.wait()
    scale = 128 ** (-0.5)

    def forward(h, carry):
        for which in range(2):
            kv_far(h, which).wait_recv()

        @pl.when(k == 1)
        def _():
            for which in range(2):
                kv_relay(h, which).start()

        for which in range(2):
            kv_near(h, which).wait_recv()
        s = dot(q[:, lanes(h)], kwin[h], LAST) * scale
        g = 1.0 / (1.0 + jnp.exp(-s))
        ok = maskf[...] > 0.0
        a = jnp.where(ok, s * g, 0.0).astype(bf16)
        att[h] = a
        slope[h] = jnp.where(ok, g * (1.0 + s * (1.0 - g)) * scale, 0.0)
        mixed[:, lanes(h)] = dot(a, vwin[h])
        return carry

    lax.fori_loop(0, HEADS, forward, 0)

    relays = []
    for d in range(1, NX):
        slot = lax.rem(x - d + NX, NX) * 2 + k
        og_sends[d - 1].wait_recv()
        relays.append(remote(og8.at[slot], og8.at[slot], ss_og.at[3 + d], rs_og.at[3 + d], partner))
        relays[-1].start()

    def norm(i, carry):
        rows = pl.ds(pl.multiple_of(i * 16, 16), 16)
        m = mixed[rows, :]
        c = m - jnp.mean(m, axis=1, keepdims=True)
        r = lax.rsqrt(jnp.mean(c * c, axis=1, keepdims=True) + 1e-05)
        n = c * r
        mixed[rows, :] = n
        inv[rows, :] = jnp.broadcast_to(r, (16, 128))
        hid[rows, :] = (n * u[rows, :].astype(f32)).astype(bf16)
        return carry

    lax.fori_loop(0, 8, norm, 0)

    for i in range(NY):
        ht[:, i] = hid[:, i * 128:i * 128 + 128].T.reshape(8, 16, 128)
    h_sends = [remote(ht.at[to_slab[r]], htr.at[me], ss_h.at[r], rs_h.at[r], xk[r]) for r in range(7)]
    for c in h_sends:
        c.start()
    htr[me] = ht[me]

    def norm_back(i, carry):
        rows = pl.ds(pl.multiple_of(i * 16, 16), 16)
        n = mixed[rows, :]
        g = gh[rows, :]
        gg_ref[rows, :] = (g * n).astype(bf16)
        gn = g * u[rows, :].astype(f32)
        gm = gn - jnp.mean(gn, axis=1, keepdims=True) - n * jnp.mean(gn * n, axis=1, keepdims=True)
        gmix[rows, :] = (gm * inv[rows, 0:1]).astype(bf16)
        return carry

    lax.fori_loop(0, 8, norm_back, 0)

    def grad_send(b, h):
        return remote(pg.at[b, h], rg.at[b, h], ss_g.at[b, h], rs_g.at[b, h], ring(-1 - b))

    def backward(h, carry):
        gm = gmix[:, lanes(h)]
        da = dot(gm, vwin[h], LAST)
        ds = (da * slope[h]).astype(bf16)
        gq_ref[:, lanes(h)] = dot(ds, kwin[h]).astype(bf16)
        gk = dot(ds, q[:, lanes(h)], FIRST)
        gv = dot(att[h], gm, FIRST)
        for which, val in enumerate((gk, gv)):
            pg[1, h, which] = val[0:128].astype(bf16)
            pg[0, h, which] = val[128:256].astype(bf16)
            go[h, which] = val[256:384]
        for b in range(2):
            grad_send(b, h).start()
        return carry

    lax.fori_loop(0, 2, backward, 0)

    for c in og_sends[3:]:
        c.wait_recv()
    for c in relays:
        c.wait_recv()
    for c in h_sends:
        c.wait_recv()
    lhs = jnp.concatenate([htr[s].reshape(128, 128) for s in range(8)], axis=1)
    for j in range(4):
        cols = slice(j * 256, j * 256 + 256)
        t = dot(lhs, og8[:, :, cols].reshape(1024, 256))
        gs[:, :, cols] = t.reshape(NY, 16, 256).astype(bf16)
    y_sends = [remote(gs.at[lax.rem(y + d, NY)], ry.at[d - 1], ss_y.at[d - 1], rs_y.at[d - 1], ys[d - 1]) for d in range(1, NY)]
    for c in y_sends:
        c.start()

    lax.fori_loop(2, 6, backward, 0)
    for c in y_sends:
        c.wait_recv()
    t = gs[y].astype(f32)
    for d in range(NY - 1):
        t = t + ry[d].astype(f32)
    for p in range(OWNERS):
        s2[p] = t[:, p * 128:p * 128 + 128].astype(bf16)

    def z_send(d):
        return remote(s2.at[lax.rem(z + d, NZ)], rz.at[d - 1], ss_z.at[d - 1], rs_z.at[d - 1], zs[d - 1])

    def a_send(d):
        return remote(ag.at[z], ag.at[z], ss_a.at[d - 1], rs_a.at[d - 1], zs[d - 1])

    for d in range(1, NZ):
        @pl.when(lax.rem(z + d, NZ) < OWNERS)
        def _():
            z_send(d).start()

    lax.fori_loop(6, HEADS, backward, 0)
    out_ref[...] = dot(hid[...], w[...]).astype(bf16)

    @pl.when(z < OWNERS)
    def _():
        for d in range(1, NZ):
            z_send(d).wait_recv()
        t = s2[z].astype(f32)
        for d in range(NZ - 1):
            t = t + rz[d].astype(f32)
        ag[z] = t.astype(bf16)
        for d in range(1, NZ):
            a_send(d).start()

    for d in range(1, NZ):
        @pl.when(lax.rem(z - d + NZ, NZ) < OWNERS)
        def _():
            a_send(d).wait_recv()

    f_sends = [remote(ag.at[pl.ds(0, OWNERS)], finr.at[me], ss_f.at[r], rs_f.at[r], xk[r]) for r in range(7)]
    for c in f_sends:
        c.start()
    finr[me] = ag[0:OWNERS]

    def grads(h, carry):
        for b in range(2):
            grad_send(b, h).wait_recv()
        gk_ref[:, lanes(h)] = (go[h, 0] + rg[0, h, 0].astype(f32) + rg[1, h, 0].astype(f32)).astype(bf16)
        gv_ref[:, lanes(h)] = (go[h, 1] + rg[0, h, 1].astype(f32) + rg[1, h, 1].astype(f32)).astype(bf16)
        return carry

    lax.fori_loop(0, HEADS, grads, 0)

    for c in f_sends:
        c.wait_recv()
    w_scale = token_total ** (-0.5)
    for s in range(8):
        for p in range(OWNERS):
            gw_ref[s * 16:s * 16 + 16, p * 128:p * 128 + 128] = finr[s, p].astype(f32) * w_scale

    def drain(h, carry):
        for which in range(2):
            kv_far(h, which).wait_send()
            kv_near(h, which).wait_send()
        for b in range(2):
            grad_send(b, h).wait_send()
        return carry

    lax.fori_loop(0, HEADS, drain, 0)
    for c in og_sends + relays + h_sends + y_sends + f_sends:
        c.wait_send()
    for d in range(1, NZ):
        @pl.when(lax.rem(z + d, NZ) < OWNERS)
        def _():
            z_send(d).wait_send()

    @pl.when(z < OWNERS)
    def _():
        for d in range(1, NZ):
            a_send(d).wait_send()


def on_device(queries, keys, values, gates, out_grad, w_out, hist_lengths):
    vm = pltpu.VMEM
    dma = pltpu.SemaphoreType.DMA
    rows, width = 128, 1024
    token_total = rows * lax.axis_size("seq") * lax.axis_size("batch")
    hbm = pl.BlockSpec(memory_space=pl.ANY)
    res = pl.BlockSpec(memory_space=pltpu.VMEM)
    outs = pl.pallas_call(
        functools.partial(layer_kernel, token_total),
        out_shape=[jax.ShapeDtypeStruct((rows, width), bf16)] * 5 + [jax.ShapeDtypeStruct((rows, width), f32)],
        in_specs=[pl.BlockSpec(memory_space=pltpu.SMEM)] + [hbm] * 6,
        out_specs=[res] * 6,
        scratch_shapes=[
            vm((rows, width), bf16), vm((rows, width), bf16), vm((width, width), bf16), vm((8, rows, width), bf16),
            vm((HEADS, 384, 128), bf16), vm((HEADS, 384, 128), bf16), vm((128, 384), f32),
            vm((HEADS, 128, 384), f32), vm((HEADS, 128, 384), bf16),
            vm((rows, width), f32), vm((rows, width), f32), vm((rows, width), bf16), vm((rows, 128), f32), vm((rows, width), bf16),
            vm((8, NY, 16, 128), bf16), vm((8, NY, 16, 128), bf16),
            vm((NY, 16, width), bf16), vm((NY - 1, 16, width), bf16),
            vm((NZ, 16, 128), bf16), vm((NZ - 1, 16, 128), bf16), vm((NZ, 16, 128), bf16),
            vm((8, OWNERS, 16, 128), bf16),
            vm((HEADS, 2, 128, 128), f32), vm((2, HEADS, 2, 128, 128), bf16), vm((2, HEADS, 2, 128, 128), bf16),
            dma((20,)), dma((2, HEADS, 2)), dma((2, HEADS, 2)), dma((7,)), dma((7,)), dma((7,)), dma((7,)),
            dma((NY - 1,)), dma((NY - 1,)), dma((NZ - 1,)), dma((NZ - 1,)), dma((NZ - 1,)), dma((NZ - 1,)),
            dma((7,)), dma((7,)), dma((2, HEADS)), dma((2, HEADS)),
        ],
        compiler_params=pltpu.CompilerParams(collective_id=0, has_side_effects=True, vmem_limit_bytes=56 << 20),
    )(hist_lengths, queries, keys, values, gates, out_grad, w_out)
    return tuple(o[None] for o in outs[:5]) + (outs[5],)


def solution(mesh):
    tokens = P("batch", "seq", None)
    return jax.shard_map(
        on_device,
        mesh=mesh,
        in_specs=(tokens,) * 5 + (P(), P("batch", None)),
        out_specs=(tokens,) * 5 + (P("batch", None),),
        check_vma=False,
    )
```

```python
import functools

import jax
import jax.numpy as jnp
from jax import lax
from jax.experimental import pallas as pl
from jax.experimental.pallas import tpu as pltpu
from jax.sharding import PartitionSpec as P

HEADS = 8
WINDOW = 256
NX, NY, NZ = 4, 8, 12
OWNERS = 8
NSEQ = NX * NZ * 2
MESH = pl.DeviceIdType.MESH
f32, bf16 = jnp.float32, jnp.bfloat16
LAST = (((1,), (1,)), ((), ()))
FIRST = (((0,), (0,)), ((), ()))


def dot(a, b, dims=(((1,), (0,)), ((), ()))):
    return lax.dot_general(a, b, dims, preferred_element_type=f32)


def layer_kernel(
    token_total, len_ref, q_hbm, k_hbm, v_hbm, u_hbm, og_hbm, w_hbm,
    out_ref, gq_ref, gk_ref, gv_ref, gg_ref, gw_ref,
    q, u, w, og8, kwin, vwin, maskf, slope, att, mixed, gh, gmix, inv, hid, ht, htr, gs, ry, s2, rz, ag, finr, go, far, pg, rg,
    ld_sem, ss_kv, rs_kv, ss_og, rs_og, ss_h, rs_h, ss_y, rs_y, ss_z, rs_z, ss_a, rs_a, ss_f, rs_f, ss_g, rs_g,
):
    seq = lax.axis_index("seq")
    y = lax.axis_index("batch")
    k = lax.rem(seq, 2)
    x = seq // (2 * NZ)
    z = lax.rem(seq // 2, NZ)
    me = x * 2 + k

    def dev(px, py, pz, pk):
        return {"seq": (px * NZ + pz) * 2 + pk, "batch": py}

    def ring(d):
        return {"seq": lax.rem(seq + d + NSEQ, NSEQ), "batch": y}

    partner = dev(x, y, z, 1 - k)
    xs = [dev(lax.rem(x + d, NX), y, z, k) for d in range(1, NX)]

    def slab_peer(r):
        s = lax.rem(me + r, 8)
        return s, dev(s // 2, y, z, lax.rem(s, 2))

    ys = [dev(x, lax.rem(y + d, NY), z, k) for d in range(1, NY)]
    zs = [dev(x, y, lax.rem(z + d, NZ), k) for d in range(1, NZ)]
    xk = [slab_peer(r)[1] for r in range(1, 8)]
    hops = [ring(-1), ring(1), ring(-2), ring(2)]

    barrier = pltpu.get_barrier_semaphore()
    greeted = xk + ys + zs + hops
    for peer in greeted:
        pl.semaphore_signal(barrier, inc=1, device_id=peer, device_id_type=MESH)

    def remote(src, dst, ss, rs, peer):
        return pltpu.make_async_remote_copy(src_ref=src, dst_ref=dst, send_sem=ss, recv_sem=rs, device_id=peer, device_id_type=MESH)

    def lanes(h):
        return pl.ds(pl.multiple_of(h * 128, 128), 128)

    loads = [
        pltpu.make_async_copy(q_hbm.at[0], q, ld_sem.at[0]),
        pltpu.make_async_copy(og_hbm.at[0], og8.at[me], ld_sem.at[1]),
        pltpu.make_async_copy(w_hbm, w, ld_sem.at[2]),
        pltpu.make_async_copy(u_hbm.at[0], u, ld_sem.at[3]),
    ]
    for h in range(HEADS):
        loads.append(pltpu.make_async_copy(k_hbm.at[0, :, pl.ds(h * 128, 128)], kwin.at[h, pl.ds(256, 128)], ld_sem.at[4 + 2 * h]))
        loads.append(pltpu.make_async_copy(v_hbm.at[0, :, pl.ds(h * 128, 128)], vwin.at[h, pl.ds(256, 128)], ld_sem.at[5 + 2 * h]))
    for c in loads:
        c.start()
    pl.semaphore_wait(barrier, len(greeted))

    def kv_far(h, which):
        ref = (kwin, vwin)[which]
        return remote(ref.at[h, pl.ds(256, 128)], ref.at[h, pl.ds(0, 128)], ss_kv.at[0, h, which], rs_kv.at[0, h, which], ring(2))

    def kv_near(h, which):
        ref = (kwin, vwin)[which]
        return remote(ref.at[h, pl.ds(256, 128)], ref.at[h, pl.ds(128, 128)], ss_kv.at[1, h, which], rs_kv.at[1, h, which], partner)

    def kv_relay(h, which):
        dst = (kwin, vwin)[which]
        return remote(dst.at[h, pl.ds(0, 128)], dst.at[h, pl.ds(128, 128)], ss_kv.at[1, h, which], rs_kv.at[1, h, which], partner)

    for c in loads[4:]:
        c.wait()
    for h in range(HEADS):
        for which in range(2):
            kv_far(h, which).start()

    @pl.when(k == 0)
    def _():
        for h in range(HEADS):
            for which in range(2):
                kv_near(h, which).start()

    def og_rows(c):
        return pl.ds(pl.multiple_of(c * 16, 16), 16)

    def og_send(d, c):
        return remote(og_hbm.at[0, og_rows(c)], og8.at[me, og_rows(c)], ss_og.at[d, c], rs_og.at[d, c], xs[d - 1] if d else partner)

    def og_block(d, c):
        return og8.at[lax.rem(x - d + NX, NX) * 2 + k, og_rows(c)]

    def og_pass(c):
        return remote(og_block(3, c), og_block(3, c), ss_og.at[2, c], rs_og.at[2, c], xs[2])

    def og_relay(d, c):
        return remote(og_block(d, c), og_block(d, c), ss_og.at[3 + d, c], rs_og.at[3 + d, c], partner)

    for c in range(8):
        og_send(3, c).start()
    for c in range(8):
        og_send(0, c).start()

    loads[1].wait()
    loads[2].wait()
    gh[...] = dot(og8[me], w[...], LAST)
    b1 = len_ref[0, 0]
    b2 = b1 + len_ref[0, 1]
    b3 = b2 + len_ref[0, 2]
    base = seq * 128
    pos = base + lax.broadcasted_iota(jnp.int32, (128, 384), 0)
    key_pos = base - 256 + lax.broadcasted_iota(jnp.int32, (128, 384), 1)
    start = jnp.where(pos >= b3, b3, jnp.where(pos >= b2, b2, jnp.where(pos >= b1, b1, 0)))
    allowed = (key_pos >= start) & (key_pos <= pos) & (key_pos > pos - WINDOW)
    maskf[...] = jnp.where(allowed, 1.0, 0.0)
    loads[0].wait()
    loads[3].wait()
    scale = 128 ** (-0.5)

    def forward(h, carry):
        for which in range(2):
            kv_far(h, which).wait_recv()

        @pl.when(k == 1)
        def _():
            for which in range(2):
                kv_relay(h, which).start()

        for which in range(2):
            kv_near(h, which).wait_recv()
        s = dot(q[:, lanes(h)], kwin[h], LAST) * scale
        g = 1.0 / (1.0 + jnp.exp(-s))
        ok = maskf[...] > 0.0
        a = jnp.where(ok, s * g, 0.0).astype(bf16)
        att[h] = a
        slope[h] = jnp.where(ok, g * (1.0 + s * (1.0 - g)) * scale, 0.0)
        mixed[:, lanes(h)] = dot(a, vwin[h])

        og_send(3, h).wait_recv()
        og_pass(h).start()
        og_relay(3, h).start()

        @pl.when(h >= 2)
        def _():
            og_pass(h - 2).wait_recv()
            og_relay(2, h - 2).start()

        @pl.when((h >= 2) & (h < 6))
        def _():
            og_send(1, 2 * h - 4).start()
            og_send(1, 2 * h - 3).start()

        return carry

    lax.fori_loop(0, HEADS, forward, 0)

    heads = [slice(h * 128, h * 128 + 128) for h in range(HEADS)]
    total = mixed[:, heads[0]]
    for h in heads[1:]:
        total = total + mixed[:, h]
    mean = jnp.broadcast_to(jnp.sum(total, axis=1, keepdims=True) * (1.0 / 1024), (128, 128))
    total = jnp.zeros((128, 128), f32)
    for h in heads:
        c = mixed[:, h] - mean
        total = total + c * c
    r = jnp.broadcast_to(lax.rsqrt(jnp.sum(total, axis=1, keepdims=True) * (1.0 / 1024) + 1e-05), (128, 128))
    inv[...] = r
    for i, h in enumerate(heads):
        n = (mixed[:, h] - mean) * r
        mixed[:, h] = n
        hd = (n * u[:, h].astype(f32)).astype(bf16)
        hid[:, h] = hd
        ht[:, i] = hd.T.reshape(8, 16, 128)

    def h_send(r):
        s, peer = slab_peer(r)
        return remote(ht.at[s], htr.at[me], ss_h.at[r - 1], rs_h.at[r - 1], peer)

    for r in range(1, 8):
        h_send(r).start()
    htr[me] = ht[me]
    for c in (6, 7):
        og_pass(c).wait_recv()
        og_relay(2, c).start()
    for c in range(8):
        og_send(1, c).wait_recv()
        og_relay(1, c).start()

    def norm_back(i, carry):
        rows = pl.ds(pl.multiple_of(i * 16, 16), 16)
        n = mixed[rows, :]
        g = gh[rows, :]
        gg_ref[rows, :] = (g * n).astype(bf16)
        gn = g * u[rows, :].astype(f32)
        gm = gn - jnp.mean(gn, axis=1, keepdims=True) - n * jnp.mean(gn * n, axis=1, keepdims=True)
        gmix[rows, :] = (gm * inv[rows, 0:1]).astype(bf16)
        return carry

    lax.fori_loop(0, 8, norm_back, 0)

    def grad_send(b, h):
        return remote(pg.at[b, h], rg.at[b, h], ss_g.at[b, h], rs_g.at[b, h], ring(-2) if b else partner)

    def backward(h, carry):
        gm = gmix[:, lanes(h)]
        da = dot(gm, vwin[h], LAST)
        ds = (da * slope[h]).astype(bf16)
        gq_ref[:, lanes(h)] = dot(ds, kwin[h]).astype(bf16)
        gk = dot(ds, q[:, lanes(h)], FIRST)
        gv = dot(att[h], gm, FIRST)
        for which, val in enumerate((gk, gv)):
            pg[0, h, which] = val[128:256].astype(bf16)
            far[h, which] = val[0:128]
            go[h, which] = val[256:384]
        grad_send(0, h).start()
        return carry

    lax.fori_loop(0, HEADS, backward, 0)
    low = (k == 0).astype(f32)
    high = (k == 1).astype(f32)

    def combine(h, carry):
        grad_send(0, h).wait_recv()
        got = rg[0, h].astype(f32)
        pg[1, h] = (far[h] + got * high).astype(bf16)
        go[h] = go[h] + got * low
        grad_send(1, h).start()
        return carry

    lax.fori_loop(0, HEADS, combine, 0)

    for c in range(8):
        og_send(0, c).wait_recv()
        for d in range(1, NX):
            og_relay(d, c).wait_recv()
    for r in range(1, 8):
        h_send(r).wait_recv()
    lhs = jnp.concatenate([htr[s].reshape(128, 128) for s in range(8)], axis=1)
    for j in range(4):
        cols = slice(j * 256, j * 256 + 256)
        t = dot(lhs, og8[:, :, cols].reshape(1024, 256))
        gs[:, :, cols] = t.reshape(NY, 16, 256).astype(bf16)
    y_sends = [remote(gs.at[lax.rem(y + d, NY)], ry.at[d - 1], ss_y.at[d - 1], rs_y.at[d - 1], ys[d - 1]) for d in range(1, NY)]
    for c in y_sends:
        c.start()

    out_ref[...] = dot(hid[...], w[...]).astype(bf16)
    for c in y_sends:
        c.wait_recv()
    t = gs[y].astype(f32)
    for d in range(NY - 1):
        t = t + ry[d].astype(f32)
    for p in range(OWNERS):
        s2[p] = t[:, p * 128:p * 128 + 128].astype(bf16)

    def z_send(d):
        return remote(s2.at[lax.rem(z + d, NZ)], rz.at[d - 1], ss_z.at[d - 1], rs_z.at[d - 1], zs[d - 1])

    def a_send(d):
        return remote(ag.at[z], ag.at[z], ss_a.at[d - 1], rs_a.at[d - 1], zs[d - 1])

    for d in range(1, NZ):
        @pl.when(lax.rem(z + d, NZ) < OWNERS)
        def _():
            z_send(d).start()

    def grads(h, carry):
        grad_send(1, h).wait_recv()
        total = go[h] + rg[1, h].astype(f32)
        gk_ref[:, lanes(h)] = total[0].astype(bf16)
        gv_ref[:, lanes(h)] = total[1].astype(bf16)
        return carry

    lax.fori_loop(0, HEADS, grads, 0)

    @pl.when(z < OWNERS)
    def _():
        for d in range(1, NZ):
            z_send(d).wait_recv()
        t = s2[z].astype(f32)
        for d in range(NZ - 1):
            t = t + rz[d].astype(f32)
        ag[z] = t.astype(bf16)
        for d in range(1, NZ):
            a_send(d).start()

    def f_send(r, p):
        return remote(ag.at[p], finr.at[me, p], ss_f.at[r - 1, p], rs_f.at[r - 1, p], slab_peer(r)[1])

    for d in (0, 1, 11, 2, 10, 3, 9, 4, 8, 5, 7, 6):
        p = lax.rem(z - d + NZ, NZ)

        @pl.when(p < OWNERS)
        def _():
            if d:
                a_send(d).wait_recv()
            finr[me, p] = ag[p]
            for r in range(1, 8):
                f_send(r, p).start()

    for r in range(1, 8):
        for p in range(OWNERS):
            f_send(r, p).wait_recv()
    w_scale = token_total ** (-0.5)
    for s in range(8):
        for p in range(OWNERS):
            gw_ref[s * 16:s * 16 + 16, p * 128:p * 128 + 128] = finr[s, p].astype(f32) * w_scale

    def drain(h, carry):
        for which in range(2):
            kv_far(h, which).wait_send()
            kv_near(h, which).wait_send()
        for b in range(2):
            grad_send(b, h).wait_send()
        for d in (0, 1, 3):
            og_send(d, h).wait_send()
        og_pass(h).wait_send()
        for d in range(1, NX):
            og_relay(d, h).wait_send()
        for r in range(1, 8):
            f_send(r, h).wait_send()
        return carry

    lax.fori_loop(0, HEADS, drain, 0)
    for r in range(1, 8):
        h_send(r).wait_send()
    for c in y_sends:
        c.wait_send()
    for d in range(1, NZ):
        @pl.when(lax.rem(z + d, NZ) < OWNERS)
        def _():
            z_send(d).wait_send()

    @pl.when(z < OWNERS)
    def _():
        for d in range(1, NZ):
            a_send(d).wait_send()


def finish_kernel(*refs):
    sems = refs[-1]
    copies = []
    for i in range(6):
        dst = refs[6 + i].at[0] if i < 5 else refs[6 + i]
        copies.append(pltpu.make_async_copy(refs[i], dst, sems.at[i]))
    for c in copies:
        c.start()
    for c in copies:
        c.wait()


def on_device(queries, keys, values, gates, out_grad, w_out, hist_lengths):
    vm = pltpu.VMEM
    dma = pltpu.SemaphoreType.DMA
    rows, width = 128, 1024
    token_total = rows * lax.axis_size("seq") * lax.axis_size("batch")
    hbm = pl.BlockSpec(memory_space=pl.ANY)
    res = pl.BlockSpec(memory_space=pltpu.VMEM)
    outs = pl.pallas_call(
        functools.partial(layer_kernel, token_total),
        out_shape=[vm((rows, width), bf16)] * 5 + [vm((rows, width), f32)],
        in_specs=[pl.BlockSpec(memory_space=pltpu.SMEM)] + [hbm] * 6,
        out_specs=[res] * 6,
        scratch_shapes=[
            vm((rows, width), bf16), vm((rows, width), bf16), vm((width, width), bf16), vm((8, rows, width), bf16),
            vm((HEADS, 384, 128), bf16), vm((HEADS, 384, 128), bf16), vm((128, 384), f32),
            vm((HEADS, 128, 384), f32), vm((HEADS, 128, 384), bf16),
            vm((rows, width), f32), vm((rows, width), f32), vm((rows, width), bf16), vm((rows, 128), f32), vm((rows, width), bf16),
            vm((8, NY, 16, 128), bf16), vm((8, NY, 16, 128), bf16),
            vm((NY, 16, width), bf16), vm((NY - 1, 16, width), bf16),
            vm((NZ, 16, 128), bf16), vm((NZ - 1, 16, 128), bf16), vm((NZ, 16, 128), bf16),
            vm((8, OWNERS, 16, 128), bf16),
            vm((HEADS, 2, 128, 128), f32), vm((HEADS, 2, 128, 128), f32), vm((2, HEADS, 2, 128, 128), bf16), vm((2, HEADS, 2, 128, 128), bf16),
            dma((20,)), dma((2, HEADS, 2)), dma((2, HEADS, 2)), dma((7, 8)), dma((7, 8)), dma((7,)), dma((7,)),
            dma((NY - 1,)), dma((NY - 1,)), dma((NZ - 1,)), dma((NZ - 1,)), dma((NZ - 1,)), dma((NZ - 1,)),
            dma((7, OWNERS)), dma((7, OWNERS)), dma((2, HEADS)), dma((2, HEADS)),
        ],
        compiler_params=pltpu.CompilerParams(collective_id=0, has_side_effects=True, vmem_limit_bytes=56 << 20),
    )(hist_lengths, queries, keys, values, gates, out_grad, w_out)
    finals = pl.pallas_call(
        finish_kernel,
        out_shape=[jax.ShapeDtypeStruct((1, rows, width), bf16)] * 5 + [jax.ShapeDtypeStruct((rows, width), f32)],
        in_specs=[hbm] * 6,
        out_specs=[hbm] * 6,
        scratch_shapes=[dma((6,))],
    )(*[pltpu.with_memory_space_constraint(o, pltpu.VMEM) for o in outs])
    return tuple(finals)


def solution(mesh):
    tokens = P("batch", "seq", None)
    return jax.shard_map(
        on_device,
        mesh=mesh,
        in_specs=(tokens,) * 5 + (P(), P("batch", None)),
        out_specs=(tokens,) * 5 + (P("batch", None),),
        check_vma=False,
    )
```

```python
import functools

import jax
import jax.numpy as jnp
from jax import lax
from jax.experimental import pallas as pl
from jax.experimental.pallas import tpu as pltpu
from jax.sharding import PartitionSpec as P

HEADS = 8
WINDOW = 256
NX, NY, NZ = 4, 8, 12
OWNERS = 8
NSEQ = NX * NZ * 2
MESH = pl.DeviceIdType.MESH
f32, bf16 = jnp.float32, jnp.bfloat16
LAST = (((1,), (1,)), ((), ()))
FIRST = (((0,), (0,)), ((), ()))


def dot(a, b, dims=(((1,), (0,)), ((), ()))):
    return lax.dot_general(a, b, dims, preferred_element_type=f32)


def layer_kernel(
    token_total, len_ref, q_hbm, k_hbm, v_hbm, u_hbm, og_hbm, w_hbm,
    out_ref, gq_ref, gk_ref, gv_ref, gg_ref, gw_ref,
    q, u, w, og8, kwin, vwin, maskf, slope, att, mixed, gh, gmix, inv, hid, ht, htr, gs, ry, s2, rz, ag, finr, go, far, pg, rg,
    news, ld_sem, ss_kv, rs_kv, ss_og, rs_og, ss_h, rs_h, ss_y, rs_y, ss_z, rs_z, ss_a, rs_a, ss_f, rs_f, ss_g, rs_g,
):
    seq = lax.axis_index("seq")
    y = lax.axis_index("batch")
    k = lax.rem(seq, 2)
    x = seq // (2 * NZ)
    z = lax.rem(seq // 2, NZ)
    me = x * 2 + k

    def dev(px, py, pz, pk):
        return {"seq": (px * NZ + pz) * 2 + pk, "batch": py}

    def ring(d):
        return {"seq": lax.rem(seq + d + NSEQ, NSEQ), "batch": y}

    partner = dev(x, y, z, 1 - k)
    xs = [dev(lax.rem(x + d, NX), y, z, k) for d in range(1, NX)]

    def slab_peer(r):
        s = lax.rem(me + r, 8)
        return s, dev(s // 2, y, z, lax.rem(s, 2))

    ys = [dev(x, lax.rem(y + d, NY), z, k) for d in range(1, NY)]
    zs = [dev(x, y, lax.rem(z + d, NZ), k) for d in range(1, NZ)]
    xk = [slab_peer(r)[1] for r in range(1, 8)]
    sides = [ys[0], ys[NY - 2], zs[0], zs[NZ - 2]]

    barrier = pltpu.get_barrier_semaphore()
    greeted = xk + sides + [ring(-2), ring(2)]
    for peer in greeted:
        pl.semaphore_signal(barrier, inc=1, device_id=peer, device_id_type=MESH)

    def remote(src, dst, ss, rs, peer):
        return pltpu.make_async_remote_copy(src_ref=src, dst_ref=dst, send_sem=ss, recv_sem=rs, device_id=peer, device_id_type=MESH)

    def lanes(h):
        return pl.ds(pl.multiple_of(h * 128, 128), 128)

    loads = [
        pltpu.make_async_copy(q_hbm.at[0], q, ld_sem.at[0]),
        pltpu.make_async_copy(og_hbm.at[0], og8.at[me], ld_sem.at[1]),
        pltpu.make_async_copy(w_hbm, w, ld_sem.at[2]),
        pltpu.make_async_copy(u_hbm.at[0], u, ld_sem.at[3]),
    ]
    for h in range(HEADS):
        loads.append(pltpu.make_async_copy(k_hbm.at[0, :, pl.ds(h * 128, 128)], kwin.at[h, pl.ds(256, 128)], ld_sem.at[4 + 2 * h]))
        loads.append(pltpu.make_async_copy(v_hbm.at[0, :, pl.ds(h * 128, 128)], vwin.at[h, pl.ds(256, 128)], ld_sem.at[5 + 2 * h]))
    for c in loads:
        c.start()
    pl.semaphore_wait(barrier, len(greeted))

    def kv_far(h, which):
        ref = (kwin, vwin)[which]
        return remote(ref.at[h, pl.ds(256, 128)], ref.at[h, pl.ds(0, 128)], ss_kv.at[0, h, which], rs_kv.at[0, h, which], ring(2))

    def kv_near(h, which):
        ref = (kwin, vwin)[which]
        return remote(ref.at[h, pl.ds(256, 128)], ref.at[h, pl.ds(128, 128)], ss_kv.at[1, h, which], rs_kv.at[1, h, which], partner)

    def kv_relay(h, which):
        dst = (kwin, vwin)[which]
        return remote(dst.at[h, pl.ds(0, 128)], dst.at[h, pl.ds(128, 128)], ss_kv.at[1, h, which], rs_kv.at[1, h, which], partner)

    for c in loads[4:]:
        c.wait()
    for h in range(HEADS):
        for which in range(2):
            kv_far(h, which).start()

    @pl.when(k == 0)
    def _():
        for h in range(HEADS):
            for which in range(2):
                kv_near(h, which).start()

    def og_rows(c):
        return pl.ds(pl.multiple_of(c * 16, 16), 16)

    def og_send(d, c):
        return remote(og_hbm.at[0, og_rows(c)], og8.at[me, og_rows(c)], ss_og.at[d, c], rs_og.at[d, c], xs[d - 1] if d else partner)

    def og_block(d, c):
        return og8.at[lax.rem(x - d + NX, NX) * 2 + k, og_rows(c)]

    def og_pass(c):
        return remote(og_block(3, c), og_block(3, c), ss_og.at[2, c], rs_og.at[2, c], xs[2])

    def og_relay(d, c):
        return remote(og_block(d, c), og_block(d, c), ss_og.at[3 + d, c], rs_og.at[3 + d, c], partner)

    for c in range(8):
        og_send(3, c).start()
    for c in range(8):
        og_send(0, c).start()

    loads[1].wait()
    loads[2].wait()
    gh[...] = dot(og8[me], w[...], LAST)
    b1 = len_ref[0, 0]
    b2 = b1 + len_ref[0, 1]
    b3 = b2 + len_ref[0, 2]
    base = seq * 128
    pos = base + lax.broadcasted_iota(jnp.int32, (128, 384), 0)
    key_pos = base - 256 + lax.broadcasted_iota(jnp.int32, (128, 384), 1)
    start = jnp.where(pos >= b3, b3, jnp.where(pos >= b2, b2, jnp.where(pos >= b1, b1, 0)))
    allowed = (key_pos >= start) & (key_pos <= pos) & (key_pos > pos - WINDOW)
    maskf[...] = jnp.where(allowed, 1.0, 0.0)
    loads[0].wait()
    loads[3].wait()
    scale = 128 ** (-0.5)

    def spread(t):
        for peer in sides:
            pl.semaphore_signal(news.at[t], inc=1, device_id=peer, device_id_type=MESH)

    def forward(h, carry):
        @pl.when((h >= 1) & (h <= 5))
        def _():
            pl.semaphore_wait(news.at[h - 1], len(sides))

        @pl.when(h < 5)
        def _():
            spread(h)

        for which in range(2):
            kv_far(h, which).wait_recv()

        @pl.when(k == 1)
        def _():
            for which in range(2):
                kv_relay(h, which).start()

        for which in range(2):
            kv_near(h, which).wait_recv()
        s = dot(q[:, lanes(h)], kwin[h], LAST) * scale
        g = 1.0 / (1.0 + jnp.exp(-s))
        ok = maskf[...] > 0.0
        a = jnp.where(ok, s * g, 0.0).astype(bf16)
        att[h] = a
        slope[h] = jnp.where(ok, g * (1.0 + s * (1.0 - g)) * scale, 0.0)
        mixed[:, lanes(h)] = dot(a, vwin[h])

        og_send(3, h).wait_recv()
        og_pass(h).start()
        og_relay(3, h).start()

        @pl.when(h >= 2)
        def _():
            og_pass(h - 2).wait_recv()
            og_relay(2, h - 2).start()

        @pl.when((h >= 2) & (h < 6))
        def _():
            og_send(1, 2 * h - 4).start()
            og_send(1, 2 * h - 3).start()

        return carry

    lax.fori_loop(0, HEADS, forward, 0)

    heads = [slice(h * 128, h * 128 + 128) for h in range(HEADS)]
    total = mixed[:, heads[0]]
    for h in heads[1:]:
        total = total + mixed[:, h]
    mean = jnp.broadcast_to(jnp.sum(total, axis=1, keepdims=True) * (1.0 / 1024), (128, 128))
    total = jnp.zeros((128, 128), f32)
    for h in heads:
        c = mixed[:, h] - mean
        total = total + c * c
    r = jnp.broadcast_to(lax.rsqrt(jnp.sum(total, axis=1, keepdims=True) * (1.0 / 1024) + 1e-05), (128, 128))
    inv[...] = r
    for i, h in enumerate(heads):
        n = (mixed[:, h] - mean) * r
        mixed[:, h] = n
        hd = (n * u[:, h].astype(f32)).astype(bf16)
        hid[:, h] = hd
        ht[:, i] = hd.T.reshape(8, 16, 128)

    def h_send(r):
        s, peer = slab_peer(r)
        return remote(ht.at[s], htr.at[me], ss_h.at[r - 1], rs_h.at[r - 1], peer)

    for r in range(1, 8):
        h_send(r).start()
    htr[me] = ht[me]
    for c in (6, 7):
        og_pass(c).wait_recv()
        og_relay(2, c).start()
    for c in range(8):
        og_send(1, c).wait_recv()
        og_relay(1, c).start()

    def norm_back(i, carry):
        rows = pl.ds(pl.multiple_of(i * 16, 16), 16)
        n = mixed[rows, :]
        g = gh[rows, :]
        gg_ref[rows, :] = (g * n).astype(bf16)
        gn = g * u[rows, :].astype(f32)
        gm = gn - jnp.mean(gn, axis=1, keepdims=True) - n * jnp.mean(gn * n, axis=1, keepdims=True)
        gmix[rows, :] = (gm * inv[rows, 0:1]).astype(bf16)
        return carry

    lax.fori_loop(0, 8, norm_back, 0)

    def grad_send(b, h):
        return remote(pg.at[b, h], rg.at[b, h], ss_g.at[b, h], rs_g.at[b, h], ring(-2) if b else partner)

    def backward(h, carry):
        gm = gmix[:, lanes(h)]
        da = dot(gm, vwin[h], LAST)
        ds = (da * slope[h]).astype(bf16)
        gq_ref[:, lanes(h)] = dot(ds, kwin[h]).astype(bf16)
        gk = dot(ds, q[:, lanes(h)], FIRST)
        gv = dot(att[h], gm, FIRST)
        for which, val in enumerate((gk, gv)):
            pg[0, h, which] = val[128:256].astype(bf16)
            far[h, which] = val[0:128]
            go[h, which] = val[256:384]
        grad_send(0, h).start()
        return carry

    lax.fori_loop(0, HEADS, backward, 0)
    low = (k == 0).astype(f32)
    high = (k == 1).astype(f32)

    def combine(h, carry):
        grad_send(0, h).wait_recv()
        got = rg[0, h].astype(f32)
        pg[1, h] = (far[h] + got * high).astype(bf16)
        go[h] = go[h] + got * low
        grad_send(1, h).start()
        return carry

    lax.fori_loop(0, HEADS, combine, 0)

    for c in range(8):
        og_send(0, c).wait_recv()
        for d in range(1, NX):
            og_relay(d, c).wait_recv()
    for r in range(1, 8):
        h_send(r).wait_recv()
    lhs = jnp.concatenate([htr[s].reshape(128, 128) for s in range(8)], axis=1)
    for j in range(4):
        cols = slice(j * 256, j * 256 + 256)
        t = dot(lhs, og8[:, :, cols].reshape(1024, 256))
        gs[:, :, cols] = t.reshape(NY, 16, 256).astype(bf16)
    y_sends = [remote(gs.at[lax.rem(y + d, NY)], ry.at[d - 1], ss_y.at[d - 1], rs_y.at[d - 1], ys[d - 1]) for d in range(1, NY)]
    for c in y_sends:
        c.start()

    out_ref[...] = dot(hid[...], w[...]).astype(bf16)
    for c in y_sends:
        c.wait_recv()
    t = gs[y].astype(f32)
    for d in range(NY - 1):
        t = t + ry[d].astype(f32)
    for p in range(OWNERS):
        s2[p] = t[:, p * 128:p * 128 + 128].astype(bf16)

    def z_send(d):
        return remote(s2.at[lax.rem(z + d, NZ)], rz.at[d - 1], ss_z.at[d - 1], rs_z.at[d - 1], zs[d - 1])

    def a_send(d):
        return remote(ag.at[z], ag.at[z], ss_a.at[d - 1], rs_a.at[d - 1], zs[d - 1])

    for d in range(1, NZ):
        @pl.when(lax.rem(z + d, NZ) < OWNERS)
        def _():
            z_send(d).start()

    def grads(h, carry):
        grad_send(1, h).wait_recv()
        total = go[h] + rg[1, h].astype(f32)
        gk_ref[:, lanes(h)] = total[0].astype(bf16)
        gv_ref[:, lanes(h)] = total[1].astype(bf16)
        return carry

    lax.fori_loop(0, HEADS, grads, 0)

    @pl.when(z < OWNERS)
    def _():
        for d in range(1, NZ):
            z_send(d).wait_recv()
        t = s2[z].astype(f32)
        for d in range(NZ - 1):
            t = t + rz[d].astype(f32)
        ag[z] = t.astype(bf16)
        for d in range(1, NZ):
            a_send(d).start()

    def f_send(r, p):
        return remote(ag.at[p], finr.at[me, p], ss_f.at[r - 1, p], rs_f.at[r - 1, p], slab_peer(r)[1])

    for d in (0, 1, 11, 2, 10, 3, 9, 4, 8, 5, 7, 6):
        p = lax.rem(z - d + NZ, NZ)

        @pl.when(p < OWNERS)
        def _():
            if d:
                a_send(d).wait_recv()
            finr[me, p] = ag[p]
            for r in range(1, 8):
                f_send(r, p).start()

    for r in range(1, 8):
        for p in range(OWNERS):
            f_send(r, p).wait_recv()
    w_scale = token_total ** (-0.5)
    for s in range(8):
        for p in range(OWNERS):
            gw_ref[s * 16:s * 16 + 16, p * 128:p * 128 + 128] = finr[s, p].astype(f32) * w_scale

    def drain(h, carry):
        for which in range(2):
            kv_far(h, which).wait_send()
            kv_near(h, which).wait_send()
        for b in range(2):
            grad_send(b, h).wait_send()
        for d in (0, 1, 3):
            og_send(d, h).wait_send()
        og_pass(h).wait_send()
        for d in range(1, NX):
            og_relay(d, h).wait_send()
        for r in range(1, 8):
            f_send(r, h).wait_send()
        return carry

    lax.fori_loop(0, HEADS, drain, 0)
    for r in range(1, 8):
        h_send(r).wait_send()
    for c in y_sends:
        c.wait_send()
    for d in range(1, NZ):
        @pl.when(lax.rem(z + d, NZ) < OWNERS)
        def _():
            z_send(d).wait_send()

    @pl.when(z < OWNERS)
    def _():
        for d in range(1, NZ):
            a_send(d).wait_send()


def finish_kernel(*refs):
    sems = refs[-1]
    copies = []
    for i in range(6):
        dst = refs[6 + i].at[0] if i < 5 else refs[6 + i]
        copies.append(pltpu.make_async_copy(refs[i], dst, sems.at[i]))
    for c in copies:
        c.start()
    for c in copies:
        c.wait()


def on_device(queries, keys, values, gates, out_grad, w_out, hist_lengths):
    vm = pltpu.VMEM
    dma = pltpu.SemaphoreType.DMA
    rows, width = 128, 1024
    token_total = rows * lax.axis_size("seq") * lax.axis_size("batch")
    hbm = pl.BlockSpec(memory_space=pl.ANY)
    res = pl.BlockSpec(memory_space=pltpu.VMEM)
    outs = pl.pallas_call(
        functools.partial(layer_kernel, token_total),
        out_shape=[vm((rows, width), bf16)] * 5 + [vm((rows, width), f32)],
        in_specs=[pl.BlockSpec(memory_space=pltpu.SMEM)] + [hbm] * 6,
        out_specs=[res] * 6,
        scratch_shapes=[
            vm((rows, width), bf16), vm((rows, width), bf16), vm((width, width), bf16), vm((8, rows, width), bf16),
            vm((HEADS, 384, 128), bf16), vm((HEADS, 384, 128), bf16), vm((128, 384), f32),
            vm((HEADS, 128, 384), f32), vm((HEADS, 128, 384), bf16),
            vm((rows, width), f32), vm((rows, width), f32), vm((rows, width), bf16), vm((rows, 128), f32), vm((rows, width), bf16),
            vm((8, NY, 16, 128), bf16), vm((8, NY, 16, 128), bf16),
            vm((NY, 16, width), bf16), vm((NY - 1, 16, width), bf16),
            vm((NZ, 16, 128), bf16), vm((NZ - 1, 16, 128), bf16), vm((NZ, 16, 128), bf16),
            vm((8, OWNERS, 16, 128), bf16),
            vm((HEADS, 2, 128, 128), f32), vm((HEADS, 2, 128, 128), f32), vm((2, HEADS, 2, 128, 128), bf16), vm((2, HEADS, 2, 128, 128), bf16),
            pltpu.SemaphoreType.REGULAR((5,)), dma((20,)), dma((2, HEADS, 2)), dma((2, HEADS, 2)), dma((7, 8)), dma((7, 8)), dma((7,)), dma((7,)),
            dma((NY - 1,)), dma((NY - 1,)), dma((NZ - 1,)), dma((NZ - 1,)), dma((NZ - 1,)), dma((NZ - 1,)),
            dma((7, OWNERS)), dma((7, OWNERS)), dma((2, HEADS)), dma((2, HEADS)),
        ],
        compiler_params=pltpu.CompilerParams(collective_id=0, has_side_effects=True, vmem_limit_bytes=56 << 20),
    )(hist_lengths, queries, keys, values, gates, out_grad, w_out)
    finals = pl.pallas_call(
        finish_kernel,
        out_shape=[jax.ShapeDtypeStruct((1, rows, width), bf16)] * 5 + [jax.ShapeDtypeStruct((rows, width), f32)],
        in_specs=[hbm] * 6,
        out_specs=[hbm] * 6,
        scratch_shapes=[dma((6,))],
    )(*[pltpu.with_memory_space_constraint(o, pltpu.VMEM) for o in outs])
    return tuple(finals)


def solution(mesh):
    tokens = P("batch", "seq", None)
    return jax.shard_map(
        on_device,
        mesh=mesh,
        in_specs=(tokens,) * 5 + (P(), P("batch", None)),
        out_specs=(tokens,) * 5 + (P("batch", None),),
        check_vma=False,
    )
```

```python
import functools

import jax
import jax.numpy as jnp
from jax import lax
from jax.experimental import pallas as pl
from jax.experimental.pallas import tpu as pltpu
from jax.sharding import PartitionSpec as P

HEADS = 8
WINDOW = 256
NX, NY, NZ = 4, 8, 12
OWNERS = 8
NSEQ = NX * NZ * 2
MESH = pl.DeviceIdType.MESH
f32, bf16 = jnp.float32, jnp.bfloat16
LAST = (((1,), (1,)), ((), ()))
FIRST = (((0,), (0,)), ((), ()))


def dot(a, b, dims=(((1,), (0,)), ((), ()))):
    return lax.dot_general(a, b, dims, preferred_element_type=f32)


def layer_kernel(
    token_total, len_hbm, q_hbm, k_hbm, v_hbm, u_hbm, og_hbm, w_hbm,
    out_ref, gq_ref, gk_ref, gv_ref, gg_ref, gw_ref,
    q, u, w, og8, kwin, vwin, maskf, slope, att, mixed, gh, gmix, inv, hid, ht, htr, gs, ry, s2, rz, ag, finr, go, far, pg, rg,
    len_ref, news, ld_sem, ss_kv, rs_kv, ss_og, rs_og, ss_h, rs_h, ss_y, rs_y, ss_z, rs_z, ss_a, rs_a, ss_f, rs_f, ss_g, rs_g,
):
    seq = lax.axis_index("seq")
    y = lax.axis_index("batch")
    k = lax.rem(seq, 2)
    x = seq // (2 * NZ)
    z = lax.rem(seq // 2, NZ)
    me = x * 2 + k

    def dev(px, py, pz, pk):
        return {"seq": (px * NZ + pz) * 2 + pk, "batch": py}

    def ring(d):
        return {"seq": lax.rem(seq + d + NSEQ, NSEQ), "batch": y}

    partner = dev(x, y, z, 1 - k)
    xs = [dev(lax.rem(x + d, NX), y, z, k) for d in range(1, NX)]

    def slab_peer(r):
        s = lax.rem(me + r, 8)
        return s, dev(s // 2, y, z, lax.rem(s, 2))

    ys = [dev(x, lax.rem(y + d, NY), z, k) for d in range(1, NY)]
    zs = [dev(x, y, lax.rem(z + d, NZ), k) for d in range(1, NZ)]
    xk = [slab_peer(r)[1] for r in range(1, 8)]
    sides = [ys[0], ys[NY - 2], zs[0], zs[NZ - 2]]

    barrier = pltpu.get_barrier_semaphore()
    greeted = xk + sides + [ring(-2), ring(2)]
    for peer in greeted:
        pl.semaphore_signal(barrier, inc=1, device_id=peer, device_id_type=MESH)

    def remote(src, dst, ss, rs, peer):
        return pltpu.make_async_remote_copy(src_ref=src, dst_ref=dst, send_sem=ss, recv_sem=rs, device_id=peer, device_id_type=MESH)

    def lanes(h):
        return pl.ds(pl.multiple_of(h * 128, 128), 128)

    loads = [
        pltpu.make_async_copy(q_hbm.at[0], q, ld_sem.at[0]),
        pltpu.make_async_copy(og_hbm.at[0], og8.at[me], ld_sem.at[1]),
        pltpu.make_async_copy(w_hbm, w, ld_sem.at[2]),
        pltpu.make_async_copy(u_hbm.at[0], u, ld_sem.at[3]),
        pltpu.make_async_copy(len_hbm, len_ref, ld_sem.at[5]),
    ]
    for h in range(HEADS):
        loads.append(pltpu.make_async_copy(k_hbm.at[0, :, pl.ds(h * 128, 128)], kwin.at[h, pl.ds(256, 128)], ld_sem.at[4]))
        loads.append(pltpu.make_async_copy(v_hbm.at[0, :, pl.ds(h * 128, 128)], vwin.at[h, pl.ds(256, 128)], ld_sem.at[4]))
    for c in loads:
        c.start()
    pl.semaphore_wait(barrier, len(greeted))

    def kv_far(h, which):
        ref = (kwin, vwin)[which]
        return remote(ref.at[h, pl.ds(256, 128)], ref.at[h, pl.ds(0, 128)], ss_kv.at[0], rs_kv.at[0, h // 2], ring(2))

    def kv_near(h, which):
        ref = (kwin, vwin)[which]
        return remote(ref.at[h, pl.ds(256, 128)], ref.at[h, pl.ds(128, 128)], ss_kv.at[1], rs_kv.at[1, h // 2], partner)

    def kv_relay(h, which):
        dst = (kwin, vwin)[which]
        return remote(dst.at[h, pl.ds(0, 128)], dst.at[h, pl.ds(128, 128)], ss_kv.at[1], rs_kv.at[1, h // 2], partner)

    pltpu.make_async_copy(pg.at[0], pg.at[1], ld_sem.at[4]).wait()
    def arrived(ref, sem):
        remote(ref, ref, ss_kv.at[0], sem, partner).wait_recv()

    def left(ref, sem):
        remote(ref, ref, sem, rs_kv.at[0, 0], partner).wait_send()

    pair = pg.at[0, pl.ds(0, 2)]
    for h in range(HEADS):
        for which in range(2):
            kv_far(h, which).start()

    @pl.when(k == 0)
    def _():
        for h in range(HEADS):
            for which in range(2):
                kv_near(h, which).start()

    def og_rows(c):
        return pl.ds(pl.multiple_of(c * 32, 32), 32)

    def og_send(d, c):
        return remote(og_hbm.at[0, og_rows(c)], og8.at[me, og_rows(c)], ss_og, rs_og.at[8 if d == 1 else c], xs[d - 1])

    def og_slot(d):
        return lax.rem(x - d + NX, NX) * 2 + k

    def og_pass(c):
        block = og8.at[og_slot(3), og_rows(c)]
        return remote(block, block, ss_og, rs_og.at[4 + c], xs[2])

    def og_relay(d, c):
        block = og8.at[og_slot(d), og_rows(c)]
        return remote(block, block, ss_og, rs_og.at[9], partner)

    for c in range(4):
        og_send(3, c).start()
    remote(og_hbm.at[0], og8.at[me], ss_og, rs_og.at[9], partner).start()

    loads[1].wait()
    loads[2].wait()
    loads[4].wait()
    gh[...] = dot(og8[me], w[...], LAST)
    b1 = len_ref[0, 0]
    b2 = b1 + len_ref[0, 1]
    b3 = b2 + len_ref[0, 2]
    base = seq * 128
    pos = base + lax.broadcasted_iota(jnp.int32, (128, 384), 0)
    key_pos = base - 256 + lax.broadcasted_iota(jnp.int32, (128, 384), 1)
    start = jnp.where(pos >= b3, b3, jnp.where(pos >= b2, b2, jnp.where(pos >= b1, b1, 0)))
    allowed = (key_pos >= start) & (key_pos <= pos) & (key_pos > pos - WINDOW)
    maskf[...] = jnp.where(allowed, 1.0, 0.0)
    loads[0].wait()
    loads[3].wait()
    scale = 128 ** (-0.5)

    def spread(t):
        for peer in sides:
            pl.semaphore_signal(news.at[t], inc=1, device_id=peer, device_id_type=MESH)

    def forward(c, carry):
        @pl.when(c >= 1)
        def _():
            pl.semaphore_wait(news.at[c - 1], len(sides))

        spread(c)
        arrived(pair, rs_kv.at[0, c])

        @pl.when(k == 1)
        def _():
            for i in range(2):
                for which in range(2):
                    kv_relay(2 * c + i, which).start()

        arrived(pair, rs_kv.at[1, c])
        for i in range(2):
            h = 2 * c + i
            s = dot(q[:, lanes(h)], kwin[h], LAST) * scale
            g = 1.0 / (1.0 + jnp.exp(-s))
            ok = maskf[...] > 0.0
            a = jnp.where(ok, s * g, 0.0).astype(bf16)
            att[h] = a
            slope[h] = jnp.where(ok, g * (1.0 + s * (1.0 - g)) * scale, 0.0)
            mixed[:, lanes(h)] = dot(a, vwin[h])
        og_send(3, c).wait_recv()
        og_pass(c).start()
        og_relay(3, c).start()

        @pl.when(c >= 1)
        def _():
            og_pass(c - 1).wait_recv()
            og_relay(2, c - 1).start()

        @pl.when(c >= 2)
        def _():
            og_send(1, 2 * c - 4).start()
            og_send(1, 2 * c - 3).start()

        return carry

    lax.fori_loop(0, 4, forward, 0)
    pl.semaphore_wait(news.at[3], len(sides))
    spread(4)

    heads = [slice(h * 128, h * 128 + 128) for h in range(HEADS)]
    total = mixed[:, heads[0]]
    for h in heads[1:]:
        total = total + mixed[:, h]
    mean = jnp.broadcast_to(jnp.sum(total, axis=1, keepdims=True) * (1.0 / 1024), (128, 128))
    total = jnp.zeros((128, 128), f32)
    for h in heads:
        c = mixed[:, h] - mean
        total = total + c * c
    r = jnp.broadcast_to(lax.rsqrt(jnp.sum(total, axis=1, keepdims=True) * (1.0 / 1024) + 1e-05), (128, 128))
    inv[...] = r
    for i, h in enumerate(heads):
        n = (mixed[:, h] - mean) * r
        mixed[:, h] = n
        hd = (n * u[:, h].astype(f32)).astype(bf16)
        hid[:, h] = hd
        ht[:, i] = hd.T.reshape(8, 16, 128)

    def h_send(r):
        s, peer = slab_peer(r)
        return remote(ht.at[s], htr.at[me], ss_h, rs_h, peer)

    for r in (4, 3, 5, 2, 6, 7, 1):
        h_send(r).start()
    htr[me] = ht[me]
    og_pass(3).wait_recv()
    og_relay(2, 3).start()

    def norm_back(i, carry):
        rows = pl.ds(pl.multiple_of(i * 16, 16), 16)
        n = mixed[rows, :]
        g = gh[rows, :]
        gg_ref[rows, :] = (g * n).astype(bf16)
        gn = g * u[rows, :].astype(f32)
        gm = gn - jnp.mean(gn, axis=1, keepdims=True) - n * jnp.mean(gn * n, axis=1, keepdims=True)
        gmix[rows, :] = (gm * inv[rows, 0:1]).astype(bf16)
        return carry

    lax.fori_loop(0, 8, norm_back, 0)

    def grad_send(b, h):
        return remote(pg.at[b, h], rg.at[b, h], ss_g.at[b], rs_g.at[4 if b else h // 2], ring(-2) if b else partner)

    def backward(h, carry):
        gm = gmix[:, lanes(h)]
        da = dot(gm, vwin[h], LAST)
        ds = (da * slope[h]).astype(bf16)
        gq_ref[:, lanes(h)] = dot(ds, kwin[h]).astype(bf16)
        gk = dot(ds, q[:, lanes(h)], FIRST)
        gv = dot(att[h], gm, FIRST)
        for which, val in enumerate((gk, gv)):
            pg[0, h, which] = val[128:256].astype(bf16)
            far[h, which] = val[0:128]
            go[h, which] = val[256:384]
        grad_send(0, h).start()
        return carry

    lax.fori_loop(0, HEADS, backward, 0)
    arrived(og8.at[0], rs_og.at[8])
    block = og8.at[og_slot(1)]
    remote(block, block, ss_og, rs_og.at[9], partner).start()
    low = (k == 0).astype(f32)
    high = (k == 1).astype(f32)

    def combine(c, carry):
        arrived(pair, rs_g.at[c])
        for i in range(2):
            h = 2 * c + i
            got = rg[0, h].astype(f32)
            pg[1, h] = (far[h] + got * high).astype(bf16)
            go[h] = go[h] + got * low
            grad_send(1, h).start()
        return carry

    lax.fori_loop(0, 4, combine, 0)

    arrived(og8.at[pl.ds(0, 4)], rs_og.at[9])
    arrived(ht.at[pl.ds(0, 7)], rs_h)
    lhs = jnp.concatenate([htr[s].reshape(128, 128) for s in range(8)], axis=1)
    for j in range(4):
        cols = slice(j * 256, j * 256 + 256)
        t = dot(lhs, og8[:, :, cols].reshape(1024, 256))
        gs[:, :, cols] = t.reshape(NY, 16, 256).astype(bf16)
    y_sends = [remote(gs.at[lax.rem(y + d, NY)], ry.at[d - 1], ss_y, rs_y, ys[d - 1]) for d in range(1, NY)]
    for d in (4, 3, 5, 2, 6, 1, 7):
        y_sends[d - 1].start()

    out_ref[...] = dot(hid[...], w[...]).astype(bf16)
    arrived(ry, rs_y)
    t = gs[y].astype(f32)
    for d in range(NY - 1):
        t = t + ry[d].astype(f32)
    for p in range(OWNERS):
        s2[p] = t[:, p * 128:p * 128 + 128].astype(bf16)

    def z_send(d):
        return remote(s2.at[lax.rem(z + d, NZ)], rz.at[d - 1], ss_z, rs_z, zs[d - 1])

    def a_send(d):
        return remote(ag.at[z], ag.at[z], ss_a, rs_a.at[d - 1], zs[d - 1])

    pl.semaphore_wait(news.at[4], len(sides))
    far_first = (6, 5, 7, 4, 8, 3, 9, 2, 10, 1, 11)
    for d in far_first:
        @pl.when(lax.rem(z + d, NZ) < OWNERS)
        def _():
            z_send(d).start()

    arrived(rg.at[1], rs_g.at[4])

    def grads(h, carry):
        total = go[h] + rg[1, h].astype(f32)
        gk_ref[:, lanes(h)] = total[0].astype(bf16)
        gv_ref[:, lanes(h)] = total[1].astype(bf16)
        return carry

    lax.fori_loop(0, HEADS, grads, 0)

    @pl.when(z < OWNERS)
    def _():
        arrived(rz, rs_z)
        t = s2[z].astype(f32)
        for d in range(NZ - 1):
            t = t + rz[d].astype(f32)
        ag[z] = t.astype(bf16)
        for d in far_first:
            a_send(d).start()

    def f_send(r, p):
        return remote(ag.at[p], finr.at[me, p], ss_f, rs_f, slab_peer(r)[1])

    for d in (0, 1, 11, 2, 10, 3, 9, 4, 8, 5, 7, 6):
        p = lax.rem(z - d + NZ, NZ)

        @pl.when(p < OWNERS)
        def _():
            if d:
                a_send(d).wait_recv()
            finr[me, p] = ag[p]
            for r in (4, 3, 5, 2, 6, 7, 1):
                f_send(r, p).start()

    arrived(finr.at[pl.ds(0, 7)], rs_f)
    w_scale = token_total ** (-0.5)
    for s in range(8):
        for p in range(OWNERS):
            gw_ref[s * 16:s * 16 + 16, p * 128:p * 128 + 128] = finr[s, p].astype(f32) * w_scale

    for i in range(2):
        left(pg.at[0], ss_kv.at[i])
        left(pg.at[0], ss_g.at[i])
    left(og8.at[pl.ds(0, 7)], ss_og)
    left(ht.at[pl.ds(0, 7)], ss_h)
    left(gs.at[pl.ds(0, 7)], ss_y)
    left(finr.at[pl.ds(0, 7)], ss_f)

    @pl.when(z < OWNERS)
    def _():
        left(s2.at[pl.ds(0, OWNERS - 1)], ss_z)
        left(s2.at[pl.ds(0, NZ - 1)], ss_a)

    @pl.when(z >= OWNERS)
    def _():
        left(s2.at[pl.ds(0, OWNERS)], ss_z)


def finish_kernel(*refs):
    sems = refs[-1]
    copies = []
    for i in range(6):
        dst = refs[6 + i].at[0] if i < 5 else refs[6 + i]
        copies.append(pltpu.make_async_copy(refs[i], dst, sems.at[i]))
    for c in copies:
        c.start()
    for c in copies:
        c.wait()


def on_device(queries, keys, values, gates, out_grad, w_out, hist_lengths):
    vm = pltpu.VMEM
    dma = pltpu.SemaphoreType.DMA
    rows, width = 128, 1024
    token_total = rows * lax.axis_size("seq") * lax.axis_size("batch")
    hbm = pl.BlockSpec(memory_space=pl.ANY)
    res = pl.BlockSpec(memory_space=pltpu.VMEM)
    outs = pl.pallas_call(
        functools.partial(layer_kernel, token_total),
        out_shape=[vm((rows, width), bf16)] * 5 + [vm((rows, width), f32)],
        in_specs=[hbm] * 7,
        out_specs=[res] * 6,
        scratch_shapes=[
            vm((rows, width), bf16), vm((rows, width), bf16), vm((width, width), bf16), vm((8, rows, width), bf16),
            vm((HEADS, 384, 128), bf16), vm((HEADS, 384, 128), bf16), vm((128, 384), f32),
            vm((HEADS, 128, 384), f32), vm((HEADS, 128, 384), bf16),
            vm((rows, width), f32), vm((rows, width), f32), vm((rows, width), bf16), vm((rows, 128), f32), vm((rows, width), bf16),
            vm((8, NY, 16, 128), bf16), vm((8, NY, 16, 128), bf16),
            vm((NY, 16, width), bf16), vm((NY - 1, 16, width), bf16),
            vm((NZ, 16, 128), bf16), vm((NZ - 1, 16, 128), bf16), vm((NZ, 16, 128), bf16),
            vm((8, OWNERS, 16, 128), bf16),
            vm((HEADS, 2, 128, 128), f32), vm((HEADS, 2, 128, 128), f32), vm((2, HEADS, 2, 128, 128), bf16), vm((2, HEADS, 2, 128, 128), bf16),
            pltpu.SMEM((1, 4), jnp.int32), pltpu.SemaphoreType.REGULAR((5,)), dma((6,)), dma((2,)), dma((2, 4)), dma, dma((10,)), dma, dma,
            dma, dma, dma, dma, dma, dma((NZ - 1,)), dma, dma, dma((2,)), dma((5,)),
        ],
        compiler_params=pltpu.CompilerParams(collective_id=0, has_side_effects=True, vmem_limit_bytes=56 << 20),
    )(hist_lengths, queries, keys, values, gates, out_grad, w_out)
    finals = pl.pallas_call(
        finish_kernel,
        out_shape=[jax.ShapeDtypeStruct((1, rows, width), bf16)] * 5 + [jax.ShapeDtypeStruct((rows, width), f32)],
        in_specs=[hbm] * 6,
        out_specs=[hbm] * 6,
        scratch_shapes=[dma((6,))],
    )(*[pltpu.with_memory_space_constraint(o, pltpu.VMEM) for o in outs])
    return tuple(finals)


def solution(mesh):
    tokens = P("batch", "seq", None)
    return jax.shard_map(
        on_device,
        mesh=mesh,
        in_specs=(tokens,) * 5 + (P(), P("batch", None)),
        out_specs=(tokens,) * 5 + (P("batch", None),),
        check_vma=False,
    )
```

```python
import functools

import jax
import jax.numpy as jnp
from jax import lax
from jax.experimental import pallas as pl
from jax.experimental.pallas import tpu as pltpu
from jax.sharding import PartitionSpec as P

HEADS = 8
WINDOW = 256
NX, NY, NZ = 4, 8, 12
OWNERS = 8
NSEQ = NX * NZ * 2
MESH = pl.DeviceIdType.MESH
f32, bf16 = jnp.float32, jnp.bfloat16
LAST = (((1,), (1,)), ((), ()))
FIRST = (((0,), (0,)), ((), ()))


def dot(a, b, dims=(((1,), (0,)), ((), ()))):
    return lax.dot_general(a, b, dims, preferred_element_type=f32)


def layer_kernel(
    token_total, len_hbm, q_hbm, k_hbm, v_hbm, u_hbm, og_hbm, w_hbm,
    out_ref, gq_ref, gk_ref, gv_ref, gg_ref, gw_ref,
    q, u, w, og8, kwin, vwin, maskf, slope, att, mixed, gh, gmix, inv, hid, ht, htr, gs, ry, s2, rz, ag, finr, go, far, pg, rg,
    len_ref, news, ld_sem, ss_kv, rs_kv, ss_og, rs_og, ss_h, rs_h, ss_y, rs_y, ss_z, rs_z, ss_a, rs_a, ss_f, rs_f, ss_g, rs_g,
):
    seq = lax.axis_index("seq")
    y = lax.axis_index("batch")
    k = lax.rem(seq, 2)
    x = seq // (2 * NZ)
    z = lax.rem(seq // 2, NZ)
    me = x * 2 + k

    def dev(px, py, pz, pk):
        return {"seq": (px * NZ + pz) * 2 + pk, "batch": py}

    def ring(d):
        return {"seq": lax.rem(seq + d + NSEQ, NSEQ), "batch": y}

    partner = dev(x, y, z, 1 - k)
    xs = [dev(lax.rem(x + d, NX), y, z, k) for d in range(1, NX)]

    def slab_peer(r):
        s = lax.rem(me + r, 8)
        return s, dev(s // 2, y, z, lax.rem(s, 2))

    ys = [dev(x, lax.rem(y + d, NY), z, k) for d in range(1, NY)]
    zs = [dev(x, y, lax.rem(z + d, NZ), k) for d in range(1, NZ)]
    xk = [slab_peer(r)[1] for r in range(1, 8)]
    sides = [ys[0], ys[NY - 2], zs[0], zs[NZ - 2]]

    barrier = pltpu.get_barrier_semaphore()
    greeted = xk + sides + [ring(-2), ring(2)]
    for peer in greeted:
        pl.semaphore_signal(barrier, inc=1, device_id=peer, device_id_type=MESH)

    def remote(src, dst, ss, rs, peer):
        return pltpu.make_async_remote_copy(src_ref=src, dst_ref=dst, send_sem=ss, recv_sem=rs, device_id=peer, device_id_type=MESH)

    def lanes(h):
        return pl.ds(pl.multiple_of(h * 128, 128), 128)

    loads = [
        pltpu.make_async_copy(q_hbm.at[0], q, ld_sem.at[0]),
        pltpu.make_async_copy(og_hbm.at[0], og8.at[me], ld_sem.at[1]),
        pltpu.make_async_copy(w_hbm, w, ld_sem.at[2]),
        pltpu.make_async_copy(u_hbm.at[0], u, ld_sem.at[3]),
        pltpu.make_async_copy(len_hbm, len_ref, ld_sem.at[5]),
    ]
    for h in range(HEADS):
        loads.append(pltpu.make_async_copy(k_hbm.at[0, :, pl.ds(h * 128, 128)], kwin.at[h, pl.ds(256, 128)], ld_sem.at[4]))
        loads.append(pltpu.make_async_copy(v_hbm.at[0, :, pl.ds(h * 128, 128)], vwin.at[h, pl.ds(256, 128)], ld_sem.at[4]))
    for c in loads:
        c.start()
    pl.semaphore_wait(barrier, len(greeted))

    def kv_far(h, which):
        ref = (kwin, vwin)[which]
        return remote(ref.at[h, pl.ds(256, 128)], ref.at[h, pl.ds(0, 128)], ss_kv.at[0], rs_kv.at[0, h // 2], ring(2))

    def kv_near(h, which):
        ref = (kwin, vwin)[which]
        return remote(ref.at[h, pl.ds(256, 128)], ref.at[h, pl.ds(128, 128)], ss_kv.at[1], rs_kv.at[1, h // 2], partner)

    def kv_relay(h, which):
        dst = (kwin, vwin)[which]
        return remote(dst.at[h, pl.ds(0, 128)], dst.at[h, pl.ds(128, 128)], ss_kv.at[1], rs_kv.at[1, h // 2], partner)

    pltpu.make_async_copy(pg.at[0], pg.at[1], ld_sem.at[4]).wait()
    def arrived(ref, sem):
        remote(ref, ref, ss_kv.at[0], sem, partner).wait_recv()

    def left(ref, sem):
        remote(ref, ref, sem, rs_kv.at[0, 0], partner).wait_send()

    pair = pg.at[0, pl.ds(0, 2)]
    for h in range(HEADS):
        for which in range(2):
            kv_far(h, which).start()

    @pl.when(k == 0)
    def _():
        for h in range(HEADS):
            for which in range(2):
                kv_near(h, which).start()

    def og_rows(c):
        return pl.ds(pl.multiple_of(c * 32, 32), 32)

    def og_send(d, c):
        return remote(og_hbm.at[0, og_rows(c)], og8.at[me, og_rows(c)], ss_og, rs_og.at[8 if d == 1 else c], xs[d - 1])

    def og_slot(d):
        return lax.rem(x - d + NX, NX) * 2 + k

    def og_pass(c):
        block = og8.at[og_slot(3), og_rows(c)]
        return remote(block, block, ss_og, rs_og.at[4 + c], xs[2])

    def og_pass_again(c):
        block = og8.at[og_slot(2), og_rows(c)]
        return remote(block, block, ss_og, rs_og.at[8], xs[2])

    def og_relay(d, c):
        block = og8.at[og_slot(d), og_rows(c)]
        return remote(block, block, ss_og, rs_og.at[9], partner)

    for c in range(4):
        og_send(3, c).start()
    remote(og_hbm.at[0], og8.at[me], ss_og, rs_og.at[9], partner).start()

    loads[1].wait()
    loads[2].wait()
    loads[4].wait()
    gh[...] = dot(og8[me], w[...], LAST)
    b1 = len_ref[0, 0]
    b2 = b1 + len_ref[0, 1]
    b3 = b2 + len_ref[0, 2]
    base = seq * 128
    pos = base + lax.broadcasted_iota(jnp.int32, (128, 384), 0)
    key_pos = base - 256 + lax.broadcasted_iota(jnp.int32, (128, 384), 1)
    start = jnp.where(pos >= b3, b3, jnp.where(pos >= b2, b2, jnp.where(pos >= b1, b1, 0)))
    allowed = (key_pos >= start) & (key_pos <= pos) & (key_pos > pos - WINDOW)
    maskf[...] = jnp.where(allowed, 1.0, 0.0)
    loads[0].wait()
    loads[3].wait()
    scale = 128 ** (-0.5)

    def spread(t):
        for peer in sides:
            pl.semaphore_signal(news.at[t], inc=1, device_id=peer, device_id_type=MESH)

    def forward(c, carry):
        @pl.when(c >= 1)
        def _():
            pl.semaphore_wait(news.at[c - 1], len(sides))

        spread(c)
        arrived(pair, rs_kv.at[0, c])

        @pl.when(k == 1)
        def _():
            for i in range(2):
                for which in range(2):
                    kv_relay(2 * c + i, which).start()

        og_send(3, c).wait_recv()
        og_pass(c).start()
        og_relay(3, c).start()
        arrived(pair, rs_kv.at[1, c])
        for i in range(2):
            h = 2 * c + i
            s = dot(q[:, lanes(h)], kwin[h], LAST) * scale
            g = 1.0 / (1.0 + jnp.exp(-s))
            ok = maskf[...] > 0.0
            a = jnp.where(ok, s * g, 0.0).astype(bf16)
            att[h] = a
            slope[h] = jnp.where(ok, g * (1.0 + s * (1.0 - g)) * scale, 0.0)
            mixed[:, lanes(h)] = dot(a, vwin[h])

        @pl.when(c >= 2)
        def _():
            og_pass(c - 2).wait_recv()
            og_pass_again(c - 2).start()
            og_relay(2, c - 2).start()

        @pl.when(c >= 2)
        def _():
            og_send(1, c).start()

        return carry

    lax.fori_loop(0, 4, forward, 0)
    pl.semaphore_wait(news.at[3], len(sides))
    spread(4)

    heads = [slice(h * 128, h * 128 + 128) for h in range(HEADS)]
    total = mixed[:, heads[0]]
    for h in heads[1:]:
        total = total + mixed[:, h]
    mean = jnp.broadcast_to(jnp.sum(total, axis=1, keepdims=True) * (1.0 / 1024), (128, 128))
    total = jnp.zeros((128, 128), f32)
    for h in heads:
        c = mixed[:, h] - mean
        total = total + c * c
    r = jnp.broadcast_to(lax.rsqrt(jnp.sum(total, axis=1, keepdims=True) * (1.0 / 1024) + 1e-05), (128, 128))
    inv[...] = r
    for i, h in enumerate(heads):
        n = (mixed[:, h] - mean) * r
        mixed[:, h] = n
        hd = (n * u[:, h].astype(f32)).astype(bf16)
        hid[:, h] = hd
        ht[:, i] = hd.T.reshape(8, 16, 128)

    def h_send(r):
        s, peer = slab_peer(r)
        return remote(ht.at[s], htr.at[me], ss_h, rs_h, peer)

    for r in (4, 3, 5, 2, 6, 7, 1):
        h_send(r).start()
    htr[me] = ht[me]
    og_pass(2).wait_recv()
    og_relay(2, 2).start()

    def norm_back(i, carry):
        rows = pl.ds(pl.multiple_of(i * 16, 16), 16)
        n = mixed[rows, :]
        g = gh[rows, :]
        gg_ref[rows, :] = (g * n).astype(bf16)
        gn = g * u[rows, :].astype(f32)
        gm = gn - jnp.mean(gn, axis=1, keepdims=True) - n * jnp.mean(gn * n, axis=1, keepdims=True)
        gmix[rows, :] = (gm * inv[rows, 0:1]).astype(bf16)
        return carry

    lax.fori_loop(0, 8, norm_back, 0)

    def grad_send(b, h):
        return remote(pg.at[b, h], rg.at[b, h], ss_g.at[b], rs_g.at[4 if b else h // 2], ring(-2) if b else partner)

    def backward(h, carry):
        gm = gmix[:, lanes(h)]
        da = dot(gm, vwin[h], LAST)
        ds = (da * slope[h]).astype(bf16)
        gq_ref[:, lanes(h)] = dot(ds, kwin[h]).astype(bf16)
        gk = dot(ds, q[:, lanes(h)], FIRST)
        gv = dot(att[h], gm, FIRST)
        for which, val in enumerate((gk, gv)):
            pg[0, h, which] = val[128:256].astype(bf16)
            far[h, which] = val[0:128]
            go[h, which] = val[256:384]
        grad_send(0, h).start()
        return carry

    lax.fori_loop(0, HEADS, backward, 0)
    og_pass(3).wait_recv()
    og_relay(2, 3).start()
    arrived(og8.at[0], rs_og.at[8])
    block = og8.at[og_slot(1)]
    remote(block, block, ss_og, rs_og.at[9], partner).start()
    low = (k == 0).astype(f32)
    high = (k == 1).astype(f32)

    def combine(c, carry):
        arrived(pair, rs_g.at[c])
        for i in range(2):
            h = 2 * c + i
            got = rg[0, h].astype(f32)
            pg[1, h] = (far[h] + got * high).astype(bf16)
            go[h] = go[h] + got * low
            grad_send(1, h).start()
        return carry

    lax.fori_loop(0, 4, combine, 0)

    arrived(og8.at[pl.ds(0, 4)], rs_og.at[9])
    arrived(ht.at[pl.ds(0, 7)], rs_h)
    lhs = jnp.concatenate([htr[s].reshape(128, 128) for s in range(8)], axis=1)
    for j in range(4):
        cols = slice(j * 256, j * 256 + 256)
        t = dot(lhs, og8[:, :, cols].reshape(1024, 256))
        gs[:, :, cols] = t.reshape(NY, 16, 256).astype(bf16)
    y_sends = [remote(gs.at[lax.rem(y + d, NY)], ry.at[d - 1], ss_y, rs_y, ys[d - 1]) for d in range(1, NY)]
    for d in (4, 3, 5, 2, 6, 1, 7):
        y_sends[d - 1].start()

    out_ref[...] = dot(hid[...], w[...]).astype(bf16)
    arrived(ry, rs_y)
    t = gs[y].astype(f32)
    for d in range(NY - 1):
        t = t + ry[d].astype(f32)
    for p in range(OWNERS):
        s2[p] = t[:, p * 128:p * 128 + 128].astype(bf16)

    def z_send(d):
        return remote(s2.at[lax.rem(z + d, NZ)], rz.at[d - 1], ss_z, rs_z, zs[d - 1])

    def a_send(d):
        return remote(ag.at[z], ag.at[z], ss_a, rs_a.at[d - 1], zs[d - 1])

    pl.semaphore_wait(news.at[4], len(sides))
    far_first = (6, 5, 7, 4, 8, 3, 9, 2, 10, 1, 11)
    for d in far_first:
        @pl.when(lax.rem(z + d, NZ) < OWNERS)
        def _():
            z_send(d).start()


    @pl.when(z < OWNERS)
    def _():
        arrived(rz, rs_z)
        t = s2[z].astype(f32)
        for d in range(NZ - 1):
            t = t + rz[d].astype(f32)
        ag[z] = t.astype(bf16)
        for d in far_first:
            a_send(d).start()

    arrived(rg.at[1], rs_g.at[4])

    def grads(h, carry):
        total = go[h] + rg[1, h].astype(f32)
        gk_ref[:, lanes(h)] = total[0].astype(bf16)
        gv_ref[:, lanes(h)] = total[1].astype(bf16)
        return carry

    lax.fori_loop(0, HEADS, grads, 0)

    def f_send(r, p):
        return remote(ag.at[p], finr.at[me, p], ss_f, rs_f, slab_peer(r)[1])

    for d in (0, 1, 11, 2, 10, 3, 9, 4, 8, 5, 7, 6):
        p = lax.rem(z - d + NZ, NZ)

        @pl.when(p < OWNERS)
        def _():
            if d:
                a_send(d).wait_recv()
            finr[me, p] = ag[p]
            for r in (4, 3, 5, 2, 6, 7, 1):
                f_send(r, p).start()

    arrived(finr.at[pl.ds(0, 7)], rs_f)
    w_scale = token_total ** (-0.5)
    for s in range(8):
        for p in range(OWNERS):
            gw_ref[s * 16:s * 16 + 16, p * 128:p * 128 + 128] = finr[s, p].astype(f32) * w_scale

    for i in range(2):
        left(pg.at[0], ss_kv.at[i])
        left(pg.at[0], ss_g.at[i])
    left(og8.at[pl.ds(0, 7)], ss_og)
    left(ht.at[pl.ds(0, 7)], ss_h)
    left(gs.at[pl.ds(0, 7)], ss_y)
    left(finr.at[pl.ds(0, 7)], ss_f)

    @pl.when(z < OWNERS)
    def _():
        left(s2.at[pl.ds(0, OWNERS - 1)], ss_z)
        left(s2.at[pl.ds(0, NZ - 1)], ss_a)

    @pl.when(z >= OWNERS)
    def _():
        left(s2.at[pl.ds(0, OWNERS)], ss_z)


def finish_kernel(*refs):
    sems = refs[-1]
    copies = []
    for i in range(6):
        dst = refs[6 + i].at[0] if i < 5 else refs[6 + i]
        copies.append(pltpu.make_async_copy(refs[i], dst, sems.at[i]))
    for c in copies:
        c.start()
    for c in copies:
        c.wait()


def on_device(queries, keys, values, gates, out_grad, w_out, hist_lengths):
    vm = pltpu.VMEM
    dma = pltpu.SemaphoreType.DMA
    rows, width = 128, 1024
    token_total = rows * lax.axis_size("seq") * lax.axis_size("batch")
    hbm = pl.BlockSpec(memory_space=pl.ANY)
    res = pl.BlockSpec(memory_space=pltpu.VMEM)
    outs = pl.pallas_call(
        functools.partial(layer_kernel, token_total),
        out_shape=[vm((rows, width), bf16)] * 5 + [vm((rows, width), f32)],
        in_specs=[hbm] * 7,
        out_specs=[res] * 6,
        scratch_shapes=[
            vm((rows, width), bf16), vm((rows, width), bf16), vm((width, width), bf16), vm((8, rows, width), bf16),
            vm((HEADS, 384, 128), bf16), vm((HEADS, 384, 128), bf16), vm((128, 384), f32),
            vm((HEADS, 128, 384), f32), vm((HEADS, 128, 384), bf16),
            vm((rows, width), f32), vm((rows, width), f32), vm((rows, width), bf16), vm((rows, 128), f32), vm((rows, width), bf16),
            vm((8, NY, 16, 128), bf16), vm((8, NY, 16, 128), bf16),
            vm((NY, 16, width), bf16), vm((NY - 1, 16, width), bf16),
            vm((NZ, 16, 128), bf16), vm((NZ - 1, 16, 128), bf16), vm((NZ, 16, 128), bf16),
            vm((8, OWNERS, 16, 128), bf16),
            vm((HEADS, 2, 128, 128), f32), vm((HEADS, 2, 128, 128), f32), vm((2, HEADS, 2, 128, 128), bf16), vm((2, HEADS, 2, 128, 128), bf16),
            pltpu.SMEM((1, 4), jnp.int32), pltpu.SemaphoreType.REGULAR((5,)), dma((6,)), dma((2,)), dma((2, 4)), dma, dma((10,)), dma, dma,
            dma, dma, dma, dma, dma, dma((NZ - 1,)), dma, dma, dma((2,)), dma((5,)),
        ],
        compiler_params=pltpu.CompilerParams(collective_id=0, has_side_effects=True, vmem_limit_bytes=56 << 20),
    )(hist_lengths, queries, keys, values, gates, out_grad, w_out)
    finals = pl.pallas_call(
        finish_kernel,
        out_shape=[jax.ShapeDtypeStruct((1, rows, width), bf16)] * 5 + [jax.ShapeDtypeStruct((rows, width), f32)],
        in_specs=[hbm] * 6,
        out_specs=[hbm] * 6,
        scratch_shapes=[dma((6,))],
    )(*[pltpu.with_memory_space_constraint(o, pltpu.VMEM) for o in outs])
    return tuple(finals)


def solution(mesh):
    tokens = P("batch", "seq", None)
    return jax.shard_map(
        on_device,
        mesh=mesh,
        in_specs=(tokens,) * 5 + (P(), P("batch", None)),
        out_specs=(tokens,) * 5 + (P("batch", None),),
        check_vma=False,
    )
```

```python
import functools

import jax
import jax.numpy as jnp
from jax import lax
from jax.experimental import pallas as pl
from jax.experimental.pallas import tpu as pltpu
from jax.sharding import PartitionSpec as P

HEADS = 8
WINDOW = 256
NX, NY, NZ = 4, 8, 12
OWNERS = 8
NSEQ = NX * NZ * 2
MESH = pl.DeviceIdType.MESH
f32, bf16 = jnp.float32, jnp.bfloat16
LAST = (((1,), (1,)), ((), ()))
FIRST = (((0,), (0,)), ((), ()))


def dot(a, b, dims=(((1,), (0,)), ((), ()))):
    return lax.dot_general(a, b, dims, preferred_element_type=f32)


def layer_kernel(
    token_total, len_hbm, q_hbm, k_hbm, v_hbm, u_hbm, og_hbm, w_hbm,
    out_ref, gq_ref, gk_ref, gv_ref, gg_ref, gw_ref,
    q, u, w, og8, kwin, vwin, maskf, slope, att, mixed, gh, gmix, inv, hid, ht, htr, gs, ry, s2, rz, ag, finr, go, far, pg, rg,
    len_ref, news, ld_sem, ss_kv, rs_kv, ss_og, rs_og, ss_h, rs_h, ss_y, rs_y, ss_z, rs_z, ss_a, rs_a, ss_f, rs_f, ss_g, rs_g,
):
    seq = lax.axis_index("seq")
    y = lax.axis_index("batch")
    k = lax.rem(seq, 2)
    x = seq // (2 * NZ)
    z = lax.rem(seq // 2, NZ)
    me = x * 2 + k

    def dev(px, py, pz, pk):
        return {"seq": (px * NZ + pz) * 2 + pk, "batch": py}

    def ring(d):
        return {"seq": lax.rem(seq + d + NSEQ, NSEQ), "batch": y}

    partner = dev(x, y, z, 1 - k)
    xs = [dev(lax.rem(x + d, NX), y, z, k) for d in range(1, NX)]

    def slab_peer(r):
        s = lax.rem(me + r, 8)
        return s, dev(s // 2, y, z, lax.rem(s, 2))

    ys = [dev(x, lax.rem(y + d, NY), z, k) for d in range(1, NY)]
    zs = [dev(x, y, lax.rem(z + d, NZ), k) for d in range(1, NZ)]
    xk = [slab_peer(r)[1] for r in range(1, 8)]
    sides = [ys[0], ys[NY - 2], zs[0], zs[NZ - 2]]

    barrier = pltpu.get_barrier_semaphore()
    greeted = xk + sides + [ring(-2), ring(2)]
    for peer in greeted:
        pl.semaphore_signal(barrier, inc=1, device_id=peer, device_id_type=MESH)

    def remote(src, dst, ss, rs, peer):
        return pltpu.make_async_remote_copy(src_ref=src, dst_ref=dst, send_sem=ss, recv_sem=rs, device_id=peer, device_id_type=MESH)

    def lanes(h):
        return pl.ds(pl.multiple_of(h * 128, 128), 128)

    loads = [
        pltpu.make_async_copy(q_hbm.at[0], q, ld_sem.at[0]),
        pltpu.make_async_copy(og_hbm.at[0], og8.at[me], ld_sem.at[1]),
        pltpu.make_async_copy(w_hbm, w, ld_sem.at[2]),
        pltpu.make_async_copy(u_hbm.at[0], u, ld_sem.at[3]),
        pltpu.make_async_copy(len_hbm, len_ref, ld_sem.at[5]),
    ]
    for h in range(HEADS):
        loads.append(pltpu.make_async_copy(k_hbm.at[0, :, pl.ds(h * 128, 128)], kwin.at[h, pl.ds(256, 128)], ld_sem.at[4]))
        loads.append(pltpu.make_async_copy(v_hbm.at[0, :, pl.ds(h * 128, 128)], vwin.at[h, pl.ds(256, 128)], ld_sem.at[4]))
    for c in loads:
        c.start()
    pl.semaphore_wait(barrier, len(greeted))

    def kv_far(h, which):
        ref = (kwin, vwin)[which]
        return remote(ref.at[h, pl.ds(256, 128)], ref.at[h, pl.ds(0, 128)], ss_kv.at[0], rs_kv.at[0, h // 2], ring(2))

    def kv_near(h, which):
        ref = (kwin, vwin)[which]
        return remote(ref.at[h, pl.ds(256, 128)], ref.at[h, pl.ds(128, 128)], ss_kv.at[1], rs_kv.at[1, h // 2], partner)

    def kv_relay(h, which):
        dst = (kwin, vwin)[which]
        return remote(dst.at[h, pl.ds(0, 128)], dst.at[h, pl.ds(128, 128)], ss_kv.at[1], rs_kv.at[1, h // 2], partner)

    pltpu.make_async_copy(pg.at[0], pg.at[1], ld_sem.at[4]).wait()
    def arrived(ref, sem):
        remote(ref, ref, ss_kv.at[0], sem, partner).wait_recv()

    def left(ref, sem):
        remote(ref, ref, sem, rs_kv.at[0, 0], partner).wait_send()

    pair = pg.at[0, pl.ds(0, 2)]
    for h in range(HEADS):
        for which in range(2):
            kv_far(h, which).start()

    @pl.when(k == 0)
    def _():
        for h in range(HEADS):
            for which in range(2):
                kv_near(h, which).start()

    def og_rows(c):
        return pl.ds(pl.multiple_of(c * 32, 32), 32)

    def og_send(d, c):
        return remote(og_hbm.at[0, og_rows(c)], og8.at[me, og_rows(c)], ss_og, rs_og.at[8 if d == 1 else c], xs[d - 1])

    def og_slot(d):
        return lax.rem(x - d + NX, NX) * 2 + k

    def og_pass(c):
        block = og8.at[og_slot(3), og_rows(c)]
        return remote(block, block, ss_og, rs_og.at[4 + c], xs[2])

    def og_pass_again(c):
        block = og8.at[og_slot(2), og_rows(c)]
        return remote(block, block, ss_og, rs_og.at[8], xs[2])

    def og_relay(d, c):
        block = og8.at[og_slot(d), og_rows(c)]
        return remote(block, block, ss_og, rs_og.at[9], partner)

    for c in range(4):
        og_send(3, c).start()
    remote(og_hbm.at[0], og8.at[me], ss_og, rs_og.at[9], partner).start()

    loads[1].wait()
    loads[2].wait()
    loads[4].wait()
    gh[...] = dot(og8[me], w[...], LAST)
    b1 = len_ref[0, 0]
    b2 = b1 + len_ref[0, 1]
    b3 = b2 + len_ref[0, 2]
    base = seq * 128
    pos = base + lax.broadcasted_iota(jnp.int32, (128, 384), 0)
    key_pos = base - 256 + lax.broadcasted_iota(jnp.int32, (128, 384), 1)
    start = jnp.where(pos >= b3, b3, jnp.where(pos >= b2, b2, jnp.where(pos >= b1, b1, 0)))
    allowed = (key_pos >= start) & (key_pos <= pos) & (key_pos > pos - WINDOW)
    maskf[...] = jnp.where(allowed, 1.0, 0.0)
    loads[0].wait()
    loads[3].wait()
    scale = 128 ** (-0.5)

    def spread(t):
        for peer in sides:
            pl.semaphore_signal(news.at[t], inc=1, device_id=peer, device_id_type=MESH)

    def forward(c, carry):
        @pl.when(c >= 1)
        def _():
            pl.semaphore_wait(news.at[c - 1], len(sides))

        spread(c)
        arrived(pair, rs_kv.at[0, c])

        @pl.when(k == 1)
        def _():
            for i in range(2):
                for which in range(2):
                    kv_relay(2 * c + i, which).start()

        og_send(3, c).wait_recv()
        og_pass(c).start()
        og_relay(3, c).start()
        arrived(pair, rs_kv.at[1, c])
        for i in range(2):
            h = 2 * c + i
            s = dot(q[:, lanes(h)], kwin[h], LAST) * scale
            g = 1.0 / (1.0 + jnp.exp(-s))
            ok = maskf[...] > 0.0
            a = jnp.where(ok, s * g, 0.0).astype(bf16)
            att[h] = a
            slope[h] = jnp.where(ok, g * (1.0 + s * (1.0 - g)) * scale, 0.0)
            mixed[:, lanes(h)] = dot(a, vwin[h])

        @pl.when(c >= 2)
        def _():
            og_pass(c - 2).wait_recv()
            og_pass_again(c - 2).start()
            og_relay(2, c - 2).start()

        @pl.when(c >= 2)
        def _():
            og_send(1, c).start()

        return carry

    lax.fori_loop(0, 4, forward, 0)
    pl.semaphore_wait(news.at[3], len(sides))
    spread(4)

    heads = [slice(h * 128, h * 128 + 128) for h in range(HEADS)]
    total = mixed[:, heads[0]]
    for h in heads[1:]:
        total = total + mixed[:, h]
    mean = jnp.broadcast_to(jnp.sum(total, axis=1, keepdims=True) * (1.0 / 1024), (128, 128))
    total = jnp.zeros((128, 128), f32)
    for h in heads:
        c = mixed[:, h] - mean
        total = total + c * c
    r = jnp.broadcast_to(lax.rsqrt(jnp.sum(total, axis=1, keepdims=True) * (1.0 / 1024) + 1e-05), (128, 128))
    inv[...] = r
    for i, h in enumerate(heads):
        n = (mixed[:, h] - mean) * r
        mixed[:, h] = n
        hd = (n * u[:, h].astype(f32)).astype(bf16)
        hid[:, h] = hd
        ht[:, i] = hd.T.reshape(8, 16, 128)

    def h_send(r):
        s, peer = slab_peer(r)
        return remote(ht.at[s], htr.at[me], ss_h, rs_h, peer)

    for r in (4, 3, 5, 2, 6, 7, 1):
        h_send(r).start()
    htr[me] = ht[me]
    og_pass(2).wait_recv()
    og_relay(2, 2).start()

    def norm_back(i, carry):
        rows = pl.ds(pl.multiple_of(i * 16, 16), 16)
        n = mixed[rows, :]
        g = gh[rows, :]
        gg_ref[rows, :] = (g * n).astype(bf16)
        gn = g * u[rows, :].astype(f32)
        gm = gn - jnp.mean(gn, axis=1, keepdims=True) - n * jnp.mean(gn * n, axis=1, keepdims=True)
        gmix[rows, :] = (gm * inv[rows, 0:1]).astype(bf16)
        return carry

    lax.fori_loop(0, 8, norm_back, 0)

    def grad_send(b, h):
        return remote(pg.at[b, h], rg.at[b, h], ss_g.at[b], rs_g.at[4 if b else h // 2], ring(-2) if b else partner)

    low = (k == 0).astype(f32)
    high = (k == 1).astype(f32)

    def combine(c):
        arrived(pair, rs_g.at[c])
        for i in range(2):
            h = 2 * c + i
            got = rg[0, h].astype(f32)
            pg[1, h] = (far[h] + got * high).astype(bf16)
            go[h] = go[h] + got * low
            grad_send(1, h).start()

    def backward(c, carry):
        for i in range(2):
            h = 2 * c + i
            gm = gmix[:, lanes(h)]
            da = dot(gm, vwin[h], LAST)
            ds = (da * slope[h]).astype(bf16)
            gq_ref[:, lanes(h)] = dot(ds, kwin[h]).astype(bf16)
            gk = dot(ds, q[:, lanes(h)], FIRST)
            gv = dot(att[h], gm, FIRST)
            for which, val in enumerate((gk, gv)):
                pg[0, h, which] = val[128:256].astype(bf16)
                far[h, which] = val[0:128]
                go[h, which] = val[256:384]
            grad_send(0, h).start()

        @pl.when(c >= 1)
        def _():
            combine(c - 1)

        return carry

    lax.fori_loop(0, 4, backward, 0)
    og_pass(3).wait_recv()
    og_relay(2, 3).start()
    arrived(og8.at[0], rs_og.at[8])
    block = og8.at[og_slot(1)]
    remote(block, block, ss_og, rs_og.at[9], partner).start()
    combine(3)

    arrived(og8.at[pl.ds(0, 4)], rs_og.at[9])
    arrived(ht.at[pl.ds(0, 7)], rs_h)
    lhs = jnp.concatenate([htr[s].reshape(128, 128) for s in range(8)], axis=1)
    for j in range(4):
        cols = slice(j * 256, j * 256 + 256)
        t = dot(lhs, og8[:, :, cols].reshape(1024, 256))
        gs[:, :, cols] = t.reshape(NY, 16, 256).astype(bf16)
    y_sends = [remote(gs.at[lax.rem(y + d, NY)], ry.at[d - 1], ss_y, rs_y, ys[d - 1]) for d in range(1, NY)]
    for d in (4, 3, 5, 2, 6, 1, 7):
        y_sends[d - 1].start()

    out_ref[...] = dot(hid[...], w[...]).astype(bf16)
    arrived(ry, rs_y)
    t = gs[y].astype(f32)
    for d in range(NY - 1):
        t = t + ry[d].astype(f32)
    for p in range(OWNERS):
        s2[p] = t[:, p * 128:p * 128 + 128].astype(bf16)

    def z_send(d):
        return remote(s2.at[lax.rem(z + d, NZ)], rz.at[d - 1], ss_z, rs_z, zs[d - 1])

    def a_send(d):
        return remote(ag.at[z], ag.at[z], ss_a, rs_a.at[d - 1], zs[d - 1])

    pl.semaphore_wait(news.at[4], len(sides))
    far_first = (6, 5, 7, 4, 8, 3, 9, 2, 10, 1, 11)
    for d in far_first:
        @pl.when(lax.rem(z + d, NZ) < OWNERS)
        def _():
            z_send(d).start()


    @pl.when(z < OWNERS)
    def _():
        arrived(rz, rs_z)
        t = s2[z].astype(f32)
        for d in range(NZ - 1):
            t = t + rz[d].astype(f32)
        ag[z] = t.astype(bf16)
        for d in far_first:
            a_send(d).start()

    arrived(rg.at[1], rs_g.at[4])

    def grads(h, carry):
        total = go[h] + rg[1, h].astype(f32)
        gk_ref[:, lanes(h)] = total[0].astype(bf16)
        gv_ref[:, lanes(h)] = total[1].astype(bf16)
        return carry

    lax.fori_loop(0, HEADS, grads, 0)

    def f_send(r, p):
        return remote(ag.at[p], finr.at[me, p], ss_f, rs_f, slab_peer(r)[1])

    for d in (0, 1, 11, 2, 10, 3, 9, 4, 8, 5, 7, 6):
        p = lax.rem(z - d + NZ, NZ)

        @pl.when(p < OWNERS)
        def _():
            if d:
                a_send(d).wait_recv()
            finr[me, p] = ag[p]
            for r in (4, 3, 5, 2, 6, 7, 1):
                f_send(r, p).start()

    arrived(finr.at[pl.ds(0, 7)], rs_f)
    w_scale = token_total ** (-0.5)
    for s in range(8):
        for p in range(OWNERS):
            gw_ref[s * 16:s * 16 + 16, p * 128:p * 128 + 128] = finr[s, p].astype(f32) * w_scale

    for i in range(2):
        left(pg.at[0], ss_kv.at[i])
        left(pg.at[0], ss_g.at[i])
    left(og8.at[pl.ds(0, 7)], ss_og)
    left(ht.at[pl.ds(0, 7)], ss_h)
    left(gs.at[pl.ds(0, 7)], ss_y)
    left(finr.at[pl.ds(0, 7)], ss_f)

    @pl.when(z < OWNERS)
    def _():
        left(s2.at[pl.ds(0, OWNERS - 1)], ss_z)
        left(s2.at[pl.ds(0, NZ - 1)], ss_a)

    @pl.when(z >= OWNERS)
    def _():
        left(s2.at[pl.ds(0, OWNERS)], ss_z)


def finish_kernel(*refs):
    sems = refs[-1]
    copies = []
    for i in range(6):
        dst = refs[6 + i].at[0] if i < 5 else refs[6 + i]
        copies.append(pltpu.make_async_copy(refs[i], dst, sems.at[i]))
    for c in copies:
        c.start()
    for c in copies:
        c.wait()


def on_device(queries, keys, values, gates, out_grad, w_out, hist_lengths):
    vm = pltpu.VMEM
    dma = pltpu.SemaphoreType.DMA
    rows, width = 128, 1024
    token_total = rows * lax.axis_size("seq") * lax.axis_size("batch")
    hbm = pl.BlockSpec(memory_space=pl.ANY)
    res = pl.BlockSpec(memory_space=pltpu.VMEM)
    outs = pl.pallas_call(
        functools.partial(layer_kernel, token_total),
        out_shape=[vm((rows, width), bf16)] * 5 + [vm((rows, width), f32)],
        in_specs=[hbm] * 7,
        out_specs=[res] * 6,
        scratch_shapes=[
            vm((rows, width), bf16), vm((rows, width), bf16), vm((width, width), bf16), vm((8, rows, width), bf16),
            vm((HEADS, 384, 128), bf16), vm((HEADS, 384, 128), bf16), vm((128, 384), f32),
            vm((HEADS, 128, 384), f32), vm((HEADS, 128, 384), bf16),
            vm((rows, width), f32), vm((rows, width), f32), vm((rows, width), bf16), vm((rows, 128), f32), vm((rows, width), bf16),
            vm((8, NY, 16, 128), bf16), vm((8, NY, 16, 128), bf16),
            vm((NY, 16, width), bf16), vm((NY - 1, 16, width), bf16),
            vm((NZ, 16, 128), bf16), vm((NZ - 1, 16, 128), bf16), vm((NZ, 16, 128), bf16),
            vm((8, OWNERS, 16, 128), bf16),
            vm((HEADS, 2, 128, 128), f32), vm((HEADS, 2, 128, 128), f32), vm((2, HEADS, 2, 128, 128), bf16), vm((2, HEADS, 2, 128, 128), bf16),
            pltpu.SMEM((1, 4), jnp.int32), pltpu.SemaphoreType.REGULAR((5,)), dma((6,)), dma((2,)), dma((2, 4)), dma, dma((10,)), dma, dma,
            dma, dma, dma, dma, dma, dma((NZ - 1,)), dma, dma, dma((2,)), dma((5,)),
        ],
        compiler_params=pltpu.CompilerParams(collective_id=0, has_side_effects=True, vmem_limit_bytes=56 << 20),
    )(hist_lengths, queries, keys, values, gates, out_grad, w_out)
    finals = pl.pallas_call(
        finish_kernel,
        out_shape=[jax.ShapeDtypeStruct((1, rows, width), bf16)] * 5 + [jax.ShapeDtypeStruct((rows, width), f32)],
        in_specs=[hbm] * 6,
        out_specs=[hbm] * 6,
        scratch_shapes=[dma((6,))],
    )(*[pltpu.with_memory_space_constraint(o, pltpu.VMEM) for o in outs])
    return tuple(finals)


def solution(mesh):
    tokens = P("batch", "seq", None)
    return jax.shard_map(
        on_device,
        mesh=mesh,
        in_specs=(tokens,) * 5 + (P(), P("batch", None)),
        out_specs=(tokens,) * 5 + (P("batch", None),),
        check_vma=False,
    )
```
